32 devices in a mesh: grp: 2 (over y), dev: 16 (over z, x, core).
Axes of the slice: x: 2, y: 2, z: 4, core: 2. Of those that a mesh axis runs over, the one named last changes fastest.
Arguments:
- queries: float32 [128, 1024], P(('grp', 'dev')), may hold values from -4.5 to 4.5
- documents: float32 [4096, 1024], P(('grp', 'dev')), may hold values from -0.75 to 0.75
- doc_codes: int32 [4096, 128], P(('grp', 'dev')), may hold values from 0 to 255
- codebook: float32 [256, 1024], replicated, may hold values from -0.75 to 0.75
- candidate_owner: int32 [128, 32], P(('grp', 'dev')), may hold values from 0 to 31, all different within a row; in each aligned block of 4 rows (0 to 3, 4 to 7, ...) at most 4 rows name the same one
- candidate_local: int32 [128, 32], P(('grp', 'dev')), may hold values from 0 to 127
Outputs:
- codebook_gradient: float32 [256, 1024], P('dev', 'grp')
- query_loss: float32 [128], P(('grp', 'dev'))
The draws below stay inside these ranges and needn't reach their ends.
Inputs may be any that keep to these rules, and one draw needn't show every extreme that they name: `candidate_owner`: each query names 32 different owners; among one device's 4 queries no owner is named more than 4 times, and in some device's queries one owner is named exactly 4 times.
All inputs are finite; a program needn't handle non-finite values.
Results may differ from the reference program's by a relative error of at most 0.0003.
Values sent between devices are 32-bit elements; how exact they have to be, the bound alone decides.
No kernel may reach another device: no remote copies, remote signals or barrier semaphores. Data moves between devices by JAX's collectives and lax.ppermute only.
A program may use at most 192 MiB of HBM per device.

```python
import math
import jax
import jax.numpy as jnp
import numpy as np
from jax import lax

D = 1024
M = 128
K = 256
C = 32
Q_DEV = 4
DOC_DEV = 128
SUB = 8
CAP = 4
NQ = 128
NDOCS = 4096
N_GRP = 2
N_DEV = 16


def draw_documents(key, part):
    inner = jax.random.fold_in(key, 21)
    return 0.125 * jax.random.truncated_normal(inner, -6.0, 6.0, (NDOCS, D), jnp.float32)


def draw_codebook(key, part):
    inner = jax.random.fold_in(key, 31)
    return 0.125 * jax.random.truncated_normal(inner, -6.0, 6.0, (K, D), jnp.float32)


def draw_queries(key, part):
    inner = jax.random.fold_in(key, 41)
    return 0.5 * jax.random.truncated_normal(inner, -6.0, 6.0, (NQ, D), jnp.float32)


def plant(entries, rng, smallest, largest):
    dims = entries.shape
    index_at = [jax.random.randint(jax.random.fold_in(rng, axis), (), 0, dims[axis]) for axis in range(len(dims))]
    entries = entries.at[tuple(index_at)].set(smallest)
    longest = dims.index(max(dims))
    index_at[longest] = (index_at[longest] + 1) % dims[longest]
    return entries.at[tuple(index_at)].set(largest)


def shared_out(stream_key, own, number, rows, amount, top, reach, lean):
    sequence = jax.random.permutation(stream_key, amount)
    packed, common = portions_of(amount, rows * top, reach, lean, True), portions_of(amount, rows * top, reach, lean, False)
    places = jnp.arange(amount)

    def named(sizes, offset_by):
        used = int((sizes > 0).sum())
        fixed = max(1, used // 4)
        moved = fixed + (places - fixed + offset_by * (used - fixed)) % max(1, amount - fixed)
        return jnp.zeros((amount,), jnp.int32).at[sequence[jnp.where(places < fixed, places, moved)]].set(jnp.asarray(sizes, jnp.int32))

    sizes = jnp.where(number % 4 == 0, named(packed, number // 4), named(common, number - number // 4 - 1))
    mixed = jax.random.permutation(jax.random.fold_in(own, 3), amount)
    donor, taker = mixed[0:amount // 2 * 2:2], mixed[1:amount // 2 * 2:2]
    slack = jnp.minimum(sizes[donor] - 1, reach - sizes[taker]) // 2
    slack = jnp.where((donor == sequence[0]) | (taker == sequence[0]) | (sizes[taker] == 0), 0, jnp.maximum(slack, 0))
    moved = jax.random.randint(jax.random.fold_in(own, 4), (amount // 2,), 0, 1 << 20) % (slack + 1)
    sizes = sizes.at[donor].add(-moved).at[taker].add(moved)
    members = jnp.searchsorted(jnp.cumsum(sizes), jnp.arange(rows * top), side="right").astype(jnp.int32)
    table = members.reshape(top, rows).T
    table = table[jax.random.permutation(jax.random.fold_in(own, 1), rows)]
    offset_by = jax.random.randint(jax.random.fold_in(own, 2), (rows, 1), 0, top)
    return jnp.take_along_axis(table, (jnp.arange(top)[None, :] + offset_by) % top, axis=1)


def portions_of(amount, total, bound, skew, full):
    weights = [(1 << 20) // math.isqrt(standing ** skew) + 1 for standing in range(1, amount + 1)]
    largest = bound if full else min(bound, max(-(-total // amount), total * weights[0] // sum(weights)))
    least = 1 if total - largest >= amount - 1 else 0
    given, surplus = [largest] + [least] * (amount - 1), total - largest - least * (amount - 1)
    while surplus > 0:
        free = [i for i in range(1, amount) if given[i] < largest] or [i for i in range(1, amount) if given[i] < bound]
        whole, left = sum([weights[i] for i in free]), surplus
        for i in free:
            extra = min(bound - given[i], max(1, left * weights[i] // whole), surplus)
            given[i] = given[i] + extra
            surplus = surplus - extra
    return np.array(given)


def setup_inputs(seed: int = 0) -> dict:
    arg_keys = jax.random.split(jax.random.key(seed), 7)
    queries = draw_queries(jax.random.fold_in(arg_keys[6], 71), 0)
    documents = draw_documents(jax.random.fold_in(arg_keys[6], 71), 0)
    doc_codes = plant(jax.random.randint(arg_keys[2], (NDOCS, M), 0, K), jax.random.fold_in(arg_keys[2], 1), 0, K - 1).astype(jnp.int32)
    codebook = draw_codebook(jax.random.fold_in(arg_keys[6], 71), 0)
    candidate_owner_keys = jax.random.split(jax.random.fold_in(arg_keys[4], 1), NQ // Q_DEV)
    candidate_owner_turns = jax.random.permutation(jax.random.fold_in(arg_keys[4], 3), NQ // Q_DEV)
    candidate_owner = jax.vmap(lambda own, number: shared_out(jax.random.fold_in(arg_keys[4], 2), own, number, Q_DEV, N_GRP * N_DEV, C, CAP, 2))(candidate_owner_keys, candidate_owner_turns).reshape((NQ, C))
    candidate_local = plant(jax.random.randint(arg_keys[5], (NQ, C), 0, DOC_DEV), jax.random.fold_in(arg_keys[5], 1), 0, DOC_DEV - 1).astype(jnp.int32)
    return dict(queries=queries, documents=documents, doc_codes=doc_codes, codebook=codebook, candidate_owner=candidate_owner, candidate_local=candidate_local)


def block_terms(query_block, owner_block, local_block, documents, doc_codes, codebook):
    doc_ids = owner_block * DOC_DEV + local_block
    vectors = documents[doc_ids]
    exact_score = jnp.einsum("qcd,qd->qc", vectors, query_block, precision=lax.Precision.HIGHEST)
    code_rows = doc_codes[doc_ids]
    query_parts = query_block.reshape(Q_DEV, M, SUB)
    lookup = jnp.einsum("qmj,kmj->qmk", query_parts, codebook.reshape(K, M, SUB), precision=lax.Precision.HIGHEST)
    flat_table = lookup.reshape(Q_DEV, M * K)
    flat_index = (code_rows + K * jnp.arange(M, dtype=jnp.int32)).reshape(Q_DEV, C * M).astype(jnp.int32)
    student = jnp.sum(jnp.take_along_axis(flat_table, flat_index, axis=1).reshape(Q_DEV, C, M), axis=2)
    teacher = jax.nn.softmax(exact_score, axis=-1)
    query_loss = jnp.sum(teacher * (jax.nn.log_softmax(exact_score, axis=-1) - jax.nn.log_softmax(student, axis=-1)), axis=-1)
    weight = jax.nn.softmax(student, axis=-1) - teacher
    row_index = jnp.broadcast_to(jnp.arange(Q_DEV, dtype=jnp.int32)[:, None], (Q_DEV, C * M))
    spread_weight = jnp.broadcast_to(weight[:, :, None], (Q_DEV, C, M)).reshape(Q_DEV, C * M)
    weight_table = jnp.zeros((Q_DEV, M * K), jnp.float32).at[row_index, flat_index].add(spread_weight)
    gradient = jnp.einsum("qmk,qmj->kmj", weight_table.reshape(Q_DEV, M, K), query_parts, precision=lax.Precision.HIGHEST)
    return query_loss, gradient.reshape(K, D)


def reference(queries, documents, doc_codes, codebook, candidate_owner, candidate_local):
    nblocks = NQ // Q_DEV

    def step(running, pieces):
        query_block, owner_block, local_block = pieces
        query_loss, gradient = block_terms(query_block, owner_block, local_block, documents, doc_codes, codebook)
        return running + gradient, query_loss

    pieces = (queries.reshape(nblocks, Q_DEV, D), candidate_owner.reshape(nblocks, Q_DEV, C), candidate_local.reshape(nblocks, Q_DEV, C))
    total, losses = lax.scan(step, jnp.zeros((K, D), jnp.float32), pieces)
    return total, losses.reshape(NQ)
```

```python
import functools

import jax
import jax.numpy as jnp
from jax import lax
from jax.experimental import pallas as pl
from jax.experimental.pallas import tpu as pltpu
from jax.sharding import PartitionSpec as P

D = 1024
M = 128
K = 256
C = 32
SUB = 8

LANE = 128
TILES = D // LANE
SPT = LANE // SUB
QN = 4
HALF = TILES // 2
ROWS = HALF * QN + SPT + 1
HIGHEST = lax.Precision.HIGHEST


def iota(shape, axis):
    return lax.broadcasted_iota(jnp.int32, shape, axis)


def place():
    return lax.axis_index("grp"), lax.axis_index("dev")


def pack_kernel(q_ref, codes_ref, owner_ref, local_ref, out_ref, codes_t):
    codes_t[...] = codes_ref[...].astype(jnp.float32).T
    owner, local = owner_ref[...], local_ref[...]
    diagonal = iota((C, C), 0) == iota((C, C), 1)
    row = jnp.zeros((1, LANE), jnp.float32)
    for q in range(QN):
        owner_col = jnp.sum(jnp.where(diagonal, owner[q : q + 1, :], 0), axis=1, keepdims=True)
        local_col = jnp.sum(jnp.where(diagonal, local[q : q + 1, :], 0), axis=1, keepdims=True)
        hit = owner_col + q * C == iota((C, LANE), 1)
        row += jnp.sum(
            jnp.where(hit, local_col.astype(jnp.float32), 0.0), axis=0, keepdims=True
        )
    for p in range(C):
        tile, core = (p // 16) * 4 + p % 4, p % 2
        base = p * ROWS
        for i in range(HALF):
            t = 2 * i + core
            out_ref[base + i * QN : base + (i + 1) * QN, :] = q_ref[:, t * LANE : (t + 1) * LANE]
        first = base + HALF * QN
        out_ref[first : first + SPT, :] = codes_t[tile * SPT : (tile + 1) * SPT, :]
        out_ref[first + SPT : first + SPT + 1, :] = row


def recon_kernel(codes_ref, other_ref, book_ref, out_ref, book_t, codes_t):
    core = lax.rem(lax.axis_index("dev"), 2)
    for block, ref in enumerate((codes_ref, other_ref)):
        codes_t[block * M : (block + 1) * M, :] = ref[...].T
    for i in range(HALF):
        t = 2 * i + core
        book = book_ref[:, pl.ds(pl.multiple_of(t * LANE, LANE), LANE)]
        book_t[0] = book[:LANE, :].T
        book_t[1] = book[LANE:, :].T
        for block in range(2):
            first = pl.multiple_of(block * M + t * SPT, SPT)
            rows = codes_t[pl.ds(first, SPT), :]
            for m in range(SPT):
                code = jnp.broadcast_to(rows[m : m + 1, :], (SUB, LANE))
                index = lax.bitwise_and(code, LANE - 1)
                low = jnp.take_along_axis(book_t[0, m * SUB : (m + 1) * SUB, :], index, axis=1)
                high = jnp.take_along_axis(book_t[1, m * SUB : (m + 1) * SUB, :], index, axis=1)
                out_ref[i, block, m * SUB : (m + 1) * SUB, :] = jnp.where(code >= LANE, high, low)


def query_rows(got_ref, row):
    return jnp.concatenate([got_ref[pl.ds(row + q, C, stride=ROWS), :] for q in range(QN)], axis=0)


def score_kernel(got_ref, docs_ref, other_ref, recon_ref, out_ref):
    group, dev = place()
    me = group * 16 + dev
    core = lax.rem(dev, 2)
    exact = [jnp.zeros((LANE, LANE), jnp.float32)] * 2
    student = [jnp.zeros((LANE, LANE), jnp.float32)] * 2
    for i in range(HALF):
        columns = pl.ds(pl.multiple_of((2 * i + core) * LANE, LANE), LANE)
        query = query_rows(got_ref, i * QN)
        for block, ref in enumerate((docs_ref, other_ref)):
            exact[block] += lax.dot_general(
                query, ref[:, columns], (((1,), (1,)), ((), ())),
                precision=HIGHEST, preferred_element_type=jnp.float32,
            )
            student[block] += jnp.dot(
                query, recon_ref[i, block], precision=HIGHEST, preferred_element_type=jnp.float32
            )
    asked = got_ref[pl.ds(ROWS - 1, C, stride=ROWS), :]
    lanes = iota((C, LANE), 1)
    wide = iota((LANE, LANE), 1)
    diagonal = iota((LANE, LANE), 0) == wide
    rows = []
    for block in range(2):
        owner = me if block == 0 else me + 1 - 2 * core
        local = jnp.concatenate(
            [
                jnp.sum(jnp.where(lanes == q * C + owner, asked, 0.0), axis=1, keepdims=True)
                for q in range(QN)
            ],
            axis=0,
        ).astype(jnp.int32)
        hit = wide == local
        for scores in (exact[block], student[block]):
            column = jnp.sum(jnp.where(hit, scores, 0.0), axis=1, keepdims=True)
            rows.append(jnp.sum(jnp.where(diagonal, column, 0.0), axis=0, keepdims=True))
    mine = jnp.concatenate(rows, axis=0)
    for p in range(C):
        out_ref[p] = mine


def pair_kernel(got_ref, out_ref):
    asked = got_ref[pl.ds(ROWS - 1, C, stride=ROWS), :]
    asked = jnp.concatenate([asked, jnp.zeros((LANE - C, LANE), jnp.float32)], axis=0).T
    local = jnp.concatenate([asked[q * C : (q + 1) * C, :C] for q in range(QN)], axis=1)
    local = local.astype(jnp.int32)
    for o in range(C):
        index = jnp.broadcast_to(local[o : o + 1, :], (SUB, LANE))
        for half in range(2):
            first = o * ROWS + HALF * QN + half * SUB
            codes = got_ref[first : first + SUB, :]
            out_ref[o, half * SUB : (half + 1) * SUB, :] = jnp.take_along_axis(codes, index, axis=1)


def log_parts(scores):
    top = jnp.max(scores, axis=0, keepdims=True)
    shifted = scores - top
    powers = jnp.exp(shifted)
    total = jnp.sum(powers, axis=0, keepdims=True)
    return powers / total, shifted - jnp.log(total)


def gradient_kernel(scores_ref, pairs_ref, got_ref, *refs):
    own_ref, core_ref, x_ref, both_ref, loss_ref, weight, table = refs
    group, dev = place()
    me = group * 16 + dev
    low = lax.rem(dev, 4)
    odd = lax.rem(iota((C, LANE), 0), 2) == 1

    def joined(mine, other):
        swapped = jnp.where(odd, pltpu.roll(other, 1, 0), pltpu.roll(other, C - 1, 0))
        return mine + swapped

    exact = joined(scores_ref[:, 0, :], scores_ref[:, 2, :])
    student = joined(scores_ref[:, 1, :], scores_ref[:, 3, :])
    teacher, log_teacher = log_parts(exact)
    soft, log_soft = log_parts(student)
    loss = jnp.sum(teacher * (log_teacher - log_soft), axis=0, keepdims=True)
    lanes = iota((1, LANE), 1)
    for q in range(QN):
        loss_ref[q] = jnp.sum(jnp.where(lanes == q * C + me, loss, 0.0))
    weight[...] = soft - teacher
    span = 4 * 16
    first = lax.div(dev, 4) * span
    words = [(iota((SUB, LANE), 0) + (first + v * SUB)).astype(jnp.float32) for v in range(span // SUB)]

    @pl.loop(0, SPT)
    def _(m):
        total = [jnp.zeros((SUB, LANE), jnp.float32)] * len(words)
        for o in range(C):
            code = jnp.broadcast_to(pairs_ref[o, pl.ds(m, 1), :], (SUB, LANE))
            share = jnp.broadcast_to(weight[o : o + 1, :], (SUB, LANE))
            for v, word in enumerate(words):
                total[v] += jnp.where(code == word, share, 0.0)
        for v in range(len(words)):
            table[pl.ds(pl.multiple_of(m * span + v * SUB, SUB), SUB), :] = total[v]

    row = (group * 2 + lax.div(low, 2)) * QN
    query = query_rows(got_ref, row)
    subspace = lax.div(iota((span, LANE), 1), SUB)
    result = jnp.zeros((span, LANE), jnp.float32)
    for m in range(SPT):
        product = jnp.dot(
            table[m * span : (m + 1) * span, :], query,
            precision=HIGHEST, preferred_element_type=jnp.float32,
        )
        result += jnp.where(subspace == m, product, 0.0)
    for i in range(4):
        block = result[i * 16 : (i + 1) * 16, :]
        for ref, who in ((own_ref, 0), (core_ref, 1), (x_ref, 2), (both_ref, 3)):
            @pl.when(low == (i ^ who))
            def _(ref=ref, block=block):
                ref[...] = block


def vmem(n):
    return [pl.BlockSpec(memory_space=pltpu.VMEM)] * n


def call(kernel, outs, n_in, scratch=(), out_specs=None, flops=0, moved=0):
    return pl.pallas_call(
        kernel,
        out_shape=outs,
        in_specs=vmem(n_in),
        out_specs=out_specs,
        scratch_shapes=list(scratch),
        compiler_params=pltpu.CompilerParams(vmem_limit_bytes=40 * 1024 * 1024),
        cost_estimate=pl.CostEstimate(flops=flops, bytes_accessed=moved, transcendentals=0),
    )


def f32(*shape):
    return jax.ShapeDtypeStruct(shape, jnp.float32)


def by_xor(value, bits, count):
    return lax.ppermute(value, "dev", [(i, i ^ bits) for i in range(count)])


def shards_once(queries, documents, doc_codes, codebook, candidate_owner, candidate_local):
    owners = lax.axis_size("dev")
    everyone = ("grp", "dev")
    other_docs = by_xor(documents, 1, owners)
    other_codes = by_xor(doc_codes, 1, owners)
    sent = call(
        pack_kernel, f32(C * ROWS, LANE), 4, [pltpu.VMEM((M, LANE), jnp.float32)], vmem(1)[0], 0, 1 << 20
    )(queries, doc_codes, candidate_owner, candidate_local)
    got = lax.all_to_all(
        sent.reshape(C, ROWS, 1, LANE), everyone, split_axis=0, concat_axis=0, tiled=True
    ).reshape(C * ROWS, LANE)
    recon = call(
        recon_kernel,
        f32(HALF, 2, LANE, LANE),
        3,
        [pltpu.VMEM((2, LANE, LANE), jnp.float32), pltpu.VMEM((2 * M, LANE), jnp.int32)],
        vmem(1)[0],
        1 << 22,
        1 << 21,
    )(doc_codes, other_codes, codebook)
    scores = call(score_kernel, f32(C, 4, LANE), 4, (), vmem(1)[0], 1 << 27, 1 << 21)(
        got, documents, other_docs, recon
    )
    all_scores = lax.all_to_all(scores, everyone, split_axis=0, concat_axis=0, tiled=True)
    pairs = call(pair_kernel, f32(C, SPT, LANE), 1, (), vmem(1)[0], 1 << 20, 1 << 20)(got)
    own, core, across, both, query_loss = call(
        gradient_kernel,
        (f32(16, LANE),) * 4 + (f32(QN),),
        3,
        [pltpu.VMEM((C, LANE), jnp.float32), pltpu.VMEM((SPT * 64, LANE), jnp.float32)],
        tuple(vmem(4)) + (pl.BlockSpec(memory_space=pltpu.SMEM),),
        1 << 28,
        1 << 21,
    )(all_scores, pairs, got)
    near = by_xor(jnp.stack([core, both]), 1, owners)
    far = by_xor(jnp.stack([across, near[1]]), 2, owners)
    dev = lax.axis_index("dev")
    odd_core, odd_x = lax.rem(dev, 2) == 1, lax.rem(lax.div(dev, 2), 2) == 1

    def pair(mine, other):
        return jnp.where(odd_core, jnp.concatenate([other, mine], 1), jnp.concatenate([mine, other], 1))

    here, there = pair(own, near[0]), pair(far[0], far[1])
    gradient = jnp.where(
        odd_x, jnp.concatenate([there, here], 1), jnp.concatenate([here, there], 1)
    )
    return gradient, query_loss


def slot_positions(candidate_owner, capacity):
    owner_flat = candidate_owner.reshape(-1)
    ordinal = jnp.arange(owner_flat.shape[0], dtype=jnp.int32)
    earlier = (owner_flat[None, :] == owner_flat[:, None]) & (ordinal[None, :] < ordinal[:, None])
    rank_inside = jnp.sum(earlier.astype(jnp.int32), axis=1)
    return owner_flat * capacity + rank_inside


def distill(exact_score, student):
    teacher = jax.nn.softmax(exact_score, axis=-1)
    query_loss = jnp.sum(
        teacher * (jax.nn.log_softmax(exact_score, axis=-1) - jax.nn.log_softmax(student, axis=-1)),
        axis=-1,
    )
    weight = jax.nn.softmax(student, axis=-1) - teacher
    return (query_loss, weight)


def code_onehot(code_block):
    return (code_block[:, :, None] == jnp.arange(K, dtype=jnp.int32)[None, None, :]).astype(
        jnp.float32
    )


def fetched_terms(queries, vectors, code_rows, codebook):
    query_count = queries.shape[0]
    exact_score = jnp.einsum("qcd,qd->qc", vectors, queries, precision=lax.Precision.HIGHEST)
    query_parts = queries.reshape(query_count, M, SUB)
    lookup = jnp.einsum(
        "qmj,kmj->qmk", query_parts, codebook.reshape(K, M, SUB), precision=lax.Precision.HIGHEST
    )

    def student_one(pieces):
        code_one, lookup_one = pieces
        return jnp.einsum(
            "cmk,mk->c", code_onehot(code_one), lookup_one, precision=lax.Precision.HIGHEST
        )

    student = lax.map(student_one, (code_rows, lookup))
    query_loss, weight = distill(exact_score, student)

    def table_one(pieces):
        code_one, weight_one = pieces
        return jnp.einsum(
            "cmk,c->mk", code_onehot(code_one), weight_one, precision=lax.Precision.HIGHEST
        )

    weight_table = lax.map(table_one, (code_rows, weight))
    gradient = jnp.einsum(
        "qmk,qmj->kmj", weight_table, query_parts, precision=lax.Precision.HIGHEST
    )
    return (query_loss, gradient.reshape(K, D))


def shards_any(queries, documents, doc_codes, codebook, candidate_owner, candidate_local):
    groups = lax.axis_size("grp")
    owners = lax.axis_size("dev")
    query_count = queries.shape[0]
    capacity = min(query_count, max(2, 2 * query_count * C // (groups * owners)))
    slot_count = groups * owners * capacity
    positions = slot_positions(candidate_owner, capacity)
    wanted = jnp.zeros((slot_count,), jnp.int32).at[positions].set(candidate_local.reshape(-1))
    asked = lax.all_to_all(
        lax.all_to_all(
            wanted.reshape(groups, owners, capacity), "grp", split_axis=0, concat_axis=0, tiled=True
        ),
        "dev",
        split_axis=1,
        concat_axis=1,
        tiled=True,
    )
    doc_index = asked.reshape(slot_count)
    found_rows = documents[doc_index].reshape(groups, owners, capacity, D)
    found_codes = doc_codes[doc_index].astype(jnp.float32).reshape(groups, owners, capacity, M)
    fetched, fetched_codes = (
        lax.all_to_all(
            lax.all_to_all(found_rows, "grp", split_axis=0, concat_axis=0, tiled=True),
            "dev",
            split_axis=1,
            concat_axis=1,
            tiled=True,
        ),
        lax.all_to_all(
            lax.all_to_all(found_codes, "grp", split_axis=0, concat_axis=0, tiled=True),
            "dev",
            split_axis=1,
            concat_axis=1,
            tiled=True,
        ),
    )
    vectors = fetched.reshape(slot_count, D)[positions].reshape(query_count, C, D)
    code_rows = (
        fetched_codes.reshape(slot_count, M)[positions].astype(jnp.int32).reshape(query_count, C, M)
    )
    query_loss, local_gradient = fetched_terms(queries, vectors, code_rows, codebook)
    partial_sum = lax.psum_scatter(local_gradient, "dev", scatter_dimension=0, tiled=True)
    codebook_gradient = lax.psum_scatter(partial_sum, "grp", scatter_dimension=1, tiled=True)
    return (codebook_gradient, query_loss)


def solution(mesh):
    in_specs = (
        P(("grp", "dev"), None),
        P(("grp", "dev"), None),
        P(("grp", "dev"), None),
        P(),
        P(("grp", "dev"), None),
        P(("grp", "dev"), None),
    )
    out_specs = (P("dev", "grp"), P(("grp", "dev")))

    def shards(queries, documents, *rest):
        once = dict(mesh.shape) == {"grp": 2, "dev": 16}
        once = once and queries.shape == (QN, D) and documents.shape == (LANE, D)
        return (shards_once if once else shards_any)(queries, documents, *rest)

    return jax.shard_map(shards, mesh=mesh, in_specs=in_specs, out_specs=out_specs, check_vma=False)
```

```python
import functools

import jax
import jax.numpy as jnp
from jax import lax
from jax.experimental import pallas as pl
from jax.experimental.pallas import tpu as pltpu
from jax.sharding import PartitionSpec as P

D = 1024
M = 128
K = 256
C = 32
SUB = 8

LANE = 128
TILES = D // LANE
SPT = LANE // SUB
QN = 4
HALF = TILES // 2
ROWS = HALF * QN + SPT + 1


def iota(shape, axis):
    return lax.broadcasted_iota(jnp.int32, shape, axis)


def place():
    return lax.axis_index("grp"), lax.axis_index("dev")


def fetch(pairs, sems):
    copies = [pltpu.make_async_copy(src, dst, sems.at[i]) for i, (src, dst) in enumerate(pairs)]
    for copy in copies:
        copy.start()
    for copy in copies:
        copy.wait()


def thirds(value):
    first = value.astype(jnp.bfloat16)
    rest = value - first.astype(jnp.float32)
    second = rest.astype(jnp.bfloat16)
    return first, second, (rest - second.astype(jnp.float32)).astype(jnp.bfloat16)


def dot(a, b):
    return jnp.dot(a, b, preferred_element_type=jnp.float32)


def pack_kernel(*refs):
    q_ref, codes_ref, owner_ref, local_ref = refs[5:9]
    out_ref, codes_t, sems = refs[4], refs[9], refs[10]
    fetch(list(zip(refs[:4], refs[5:9])), sems)
    codes_t[...] = codes_ref[...].astype(jnp.float32).T
    owner, local = owner_ref[...], local_ref[...]
    diagonal = iota((C, C), 0) == iota((C, C), 1)
    row = jnp.zeros((1, LANE), jnp.float32)
    for q in range(QN):
        owner_col = jnp.sum(jnp.where(diagonal, owner[q : q + 1, :], 0), axis=1, keepdims=True)
        local_col = jnp.sum(jnp.where(diagonal, local[q : q + 1, :], 0), axis=1, keepdims=True)
        hit = owner_col + q * C == iota((C, LANE), 1)
        row += jnp.sum(
            jnp.where(hit, local_col.astype(jnp.float32), 0.0), axis=0, keepdims=True
        )
    for p in range(C):
        tile, core = (p // 16) * 4 + p % 4, p % 2
        base = p * ROWS
        for i in range(HALF):
            t = 2 * i + core
            out_ref[base + i * QN : base + (i + 1) * QN, :] = q_ref[:, t * LANE : (t + 1) * LANE]
        first = base + HALF * QN
        out_ref[first : first + SPT, :] = codes_t[tile * SPT : (tile + 1) * SPT, :]
        out_ref[first + SPT : first + SPT + 1, :] = row


def owner_kernel(codes_ref, other_ref, book_ref, docs_ref, other_docs_ref, out_ref, book_t, codes_t):
    core = lax.rem(lax.axis_index("dev"), 2)

    def put(i, column, value):
        for level, part in enumerate(thirds(value)):
            out_ref[level, i * LANE : (i + 1) * LANE, column * LANE : (column + 1) * LANE] = part

    for block, ref in enumerate((codes_ref, other_ref)):
        codes_t[block * M : (block + 1) * M, :] = ref[...].T
    for i in range(HALF):
        t = 2 * i + core
        columns = pl.ds(pl.multiple_of(t * LANE, LANE), LANE)
        for block, ref in enumerate((docs_ref, other_docs_ref)):
            put(i, block, ref[:, columns].T)
        book_t[0] = book_ref[:LANE, columns].T
        book_t[1] = book_ref[LANE:, columns].T
        for block in range(2):
            first = pl.multiple_of(block * M + t * SPT, SPT)
            rows = codes_t[pl.ds(first, SPT), :]
            made = []
            for m in range(SPT):
                code = jnp.broadcast_to(rows[m : m + 1, :], (SUB, LANE))
                index = lax.bitwise_and(code, LANE - 1)
                low = jnp.take_along_axis(book_t[0, m * SUB : (m + 1) * SUB, :], index, axis=1)
                high = jnp.take_along_axis(book_t[1, m * SUB : (m + 1) * SUB, :], index, axis=1)
                made.append(jnp.where(code >= LANE, high, low))
            put(i, 2 + block, jnp.concatenate(made, axis=0))


def query_rows(got_ref, row):
    return jnp.concatenate([got_ref[pl.ds(row + q, C, stride=ROWS), :] for q in range(QN)], axis=0)


def score_kernel(got_ref, table_ref, out_ref):
    group, dev = place()
    me = group * 16 + dev
    core = lax.rem(dev, 2)
    query = jnp.concatenate([query_rows(got_ref, i * QN) for i in range(HALF)], axis=1)
    q0, q1, q2 = thirds(query)
    t0, t1, t2 = table_ref[0], table_ref[1], table_ref[2]
    scores = dot(q0, t2) + dot(q2, t0) + dot(q1, t1)
    scores = scores + (dot(q0, t1) + dot(q1, t0))
    scores = scores + dot(q0, t0)
    asked = got_ref[pl.ds(ROWS - 1, C, stride=ROWS), :]
    lanes = iota((C, LANE), 1)
    wide = iota((LANE, LANE), 1)
    diagonal = iota((LANE, LANE), 0) == wide
    rows = []
    for block in range(2):
        owner = me if block == 0 else me + 1 - 2 * core
        local = jnp.concatenate(
            [
                jnp.sum(jnp.where(lanes == q * C + owner, asked, 0.0), axis=1, keepdims=True)
                for q in range(QN)
            ],
            axis=0,
        ).astype(jnp.int32)
        hit = wide == local
        for kind in range(2):
            first = (kind * 2 + block) * LANE
            column = jnp.sum(
                jnp.where(hit, scores[:, first : first + LANE], 0.0), axis=1, keepdims=True
            )
            rows.append(jnp.sum(jnp.where(diagonal, column, 0.0), axis=0, keepdims=True))
    mine = jnp.concatenate(rows, axis=0)
    for p in range(C):
        out_ref[p] = mine


def pair_kernel(got_ref, out_ref, query_ref):
    group, dev = place()
    half = group * 2 + lax.div(lax.rem(dev, 4), 2)
    first, second, _ = thirds(query_rows(got_ref, half * QN))
    for rows in (slice(0, LANE), slice(LANE, 2 * LANE)):
        query_ref[rows, :LANE] = first
        query_ref[rows, LANE:] = second
    asked = got_ref[pl.ds(ROWS - 1, C, stride=ROWS), :]
    asked = jnp.concatenate([asked, jnp.zeros((LANE - C, LANE), jnp.float32)], axis=0).T
    local = jnp.concatenate([asked[q * C : (q + 1) * C, :C] for q in range(QN)], axis=1)
    local = local.astype(jnp.int32)
    for o in range(C):
        index = jnp.broadcast_to(local[o : o + 1, :], (SUB, LANE))
        for half in range(2):
            first = o * ROWS + HALF * QN + half * SUB
            codes = got_ref[first : first + SUB, :]
            found = jnp.take_along_axis(codes, index, axis=1)
            out_ref[o, half * SUB : (half + 1) * SUB, :] = found


def log_parts(scores):
    top = jnp.max(scores, axis=0, keepdims=True)
    shifted = scores - top
    powers = jnp.exp(shifted)
    total = jnp.sum(powers, axis=0, keepdims=True)
    return powers / total, shifted - jnp.log(total)


def gradient_kernel(scores_ref, pairs_ref, query_ref, *refs):
    own_ref, core_ref, x_ref, both_ref, loss_ref, weight, table = refs
    group, dev = place()
    me = group * 16 + dev
    low = lax.rem(dev, 4)
    odd = lax.rem(iota((C, LANE), 0), 2) == 1

    def joined(mine, other):
        swapped = jnp.where(odd, pltpu.roll(other, 1, 0), pltpu.roll(other, C - 1, 0))
        return mine + swapped

    exact = joined(scores_ref[:, 0, :], scores_ref[:, 2, :])
    student = joined(scores_ref[:, 1, :], scores_ref[:, 3, :])
    teacher, log_teacher = log_parts(exact)
    soft, log_soft = log_parts(student)
    loss = jnp.sum(teacher * (log_teacher - log_soft), axis=0, keepdims=True)
    lanes = iota((1, LANE), 1)
    for q in range(QN):
        loss_ref[q] = jnp.sum(jnp.where(lanes == q * C + me, loss, 0.0))
    share = soft - teacher
    for o in range(C):
        weight[o] = jnp.broadcast_to(share[o : o + 1, :], (SUB, LANE))
    span = 4 * 16
    first = lax.div(dev, 4) * span
    words = [(iota((SUB, LANE), 0) + (first + v * SUB)).astype(jnp.float32) for v in range(span // SUB)]

    @pl.loop(0, SPT)
    def _(m):
        total = [jnp.zeros((SUB, LANE), jnp.float32)] * len(words)
        for o in range(C):
            code = jnp.broadcast_to(pairs_ref[o, pl.ds(m, 1), :], (SUB, LANE))
            part = weight[o]
            for v, word in enumerate(words):
                total[v] += jnp.where(code == word, part, 0.0)
        rows = pl.ds(pl.multiple_of(m * span, span), span)
        first, second, _ = thirds(jnp.concatenate(total, axis=0))
        table[rows, :LANE] = first
        table[rows, LANE:] = second

    subspace = lax.div(iota((span, LANE), 1), SUB)
    product = dot(table[...], query_ref[...])
    product = product[:, :LANE] + product[:, LANE:]
    result = jnp.zeros((span, LANE), jnp.float32)
    for m in range(SPT):
        result += jnp.where(subspace == m, product[m * span : (m + 1) * span, :], 0.0)
    for i in range(4):
        block = result[i * 16 : (i + 1) * 16, :]
        for ref, who in ((own_ref, 0), (core_ref, 1), (x_ref, 2), (both_ref, 3)):
            @pl.when(low == (i ^ who))
            def _(ref=ref, block=block):
                ref[...] = block


def vmem(n):
    return [pl.BlockSpec(memory_space=pltpu.VMEM)] * n


def call(kernel, outs, n_in, scratch=(), out_specs=None, flops=0, moved=0, space=pltpu.VMEM, mib=8):
    return pl.pallas_call(
        kernel,
        out_shape=outs,
        in_specs=[pl.BlockSpec(memory_space=space)] * n_in,
        out_specs=out_specs,
        scratch_shapes=list(scratch),
        compiler_params=pltpu.CompilerParams(vmem_limit_bytes=mib * 1024 * 1024),
        cost_estimate=pl.CostEstimate(flops=flops, bytes_accessed=moved, transcendentals=0),
    )


def f32(*shape):
    return jax.ShapeDtypeStruct(shape, jnp.float32)


def by_xor(value, bits, count):
    return lax.ppermute(value, "dev", [(i, i ^ bits) for i in range(count)])


def shards_once(queries, documents, doc_codes, codebook, candidate_owner, candidate_local):
    owners = lax.axis_size("dev")
    everyone = ("grp", "dev")
    other_docs = by_xor(documents, 1, owners)
    other_codes = by_xor(doc_codes, 1, owners)
    sent = call(
        pack_kernel,
        f32(C * ROWS, LANE),
        4,
        [
            pltpu.VMEM((QN, D), jnp.float32),
            pltpu.VMEM((LANE, M), jnp.int32),
            pltpu.VMEM((QN, C), jnp.int32),
            pltpu.VMEM((QN, C), jnp.int32),
            pltpu.VMEM((M, LANE), jnp.float32),
            pltpu.SemaphoreType.DMA((4,)),
        ],
        vmem(1)[0],
        0,
        1 << 20,
        pl.ANY,
        62,
    )(queries, doc_codes, candidate_owner, candidate_local)
    got = lax.all_to_all(
        sent.reshape(C, ROWS, 1, LANE), everyone, split_axis=0, concat_axis=0, tiled=True
    ).reshape(C * ROWS, LANE)
    table = call(
        owner_kernel,
        jax.ShapeDtypeStruct((3, HALF * LANE, 4 * LANE), jnp.bfloat16),
        5,
        [pltpu.VMEM((2, LANE, LANE), jnp.float32), pltpu.VMEM((2 * M, LANE), jnp.int32)],
        vmem(1)[0],
        1 << 22,
        1 << 21,
    )(doc_codes, other_codes, codebook, documents, other_docs)
    scores = call(score_kernel, f32(C, 4, LANE), 2, (), vmem(1)[0], 1 << 27, 1 << 21)(got, table)
    all_scores = lax.all_to_all(scores, everyone, split_axis=0, concat_axis=0, tiled=True)
    pairs, columns = call(
        pair_kernel,
        (f32(C, SPT, LANE), jax.ShapeDtypeStruct((2 * LANE, 2 * LANE), jnp.bfloat16)),
        1,
        (),
        tuple(vmem(2)),
        1 << 20,
        1 << 20,
    )(got)
    own, core, across, both, query_loss = call(
        gradient_kernel,
        (f32(16, LANE),) * 4 + (f32(QN),),
        3,
        [pltpu.VMEM((C, SUB, LANE), jnp.float32), pltpu.VMEM((SPT * 64, 2 * LANE), jnp.bfloat16)],
        tuple(vmem(4)) + (pl.BlockSpec(memory_space=pltpu.SMEM),),
        1 << 28,
        1 << 21,
    )(all_scores, pairs, columns)
    near = by_xor(jnp.stack([core, both]), 1, owners)
    far = by_xor(jnp.stack([across, near[1]]), 2, owners)
    dev = lax.axis_index("dev")
    odd_core, odd_x = lax.rem(dev, 2) == 1, lax.rem(lax.div(dev, 2), 2) == 1

    def pair(mine, other):
        return jnp.where(odd_core, jnp.concatenate([other, mine], 1), jnp.concatenate([mine, other], 1))

    here, there = pair(own, near[0]), pair(far[0], far[1])
    gradient = jnp.where(
        odd_x, jnp.concatenate([there, here], 1), jnp.concatenate([here, there], 1)
    )
    return gradient, query_loss


def slot_positions(candidate_owner, capacity):
    owner_flat = candidate_owner.reshape(-1)
    ordinal = jnp.arange(owner_flat.shape[0], dtype=jnp.int32)
    earlier = (owner_flat[None, :] == owner_flat[:, None]) & (ordinal[None, :] < ordinal[:, None])
    rank_inside = jnp.sum(earlier.astype(jnp.int32), axis=1)
    return owner_flat * capacity + rank_inside


def distill(exact_score, student):
    teacher = jax.nn.softmax(exact_score, axis=-1)
    query_loss = jnp.sum(
        teacher * (jax.nn.log_softmax(exact_score, axis=-1) - jax.nn.log_softmax(student, axis=-1)),
        axis=-1,
    )
    weight = jax.nn.softmax(student, axis=-1) - teacher
    return (query_loss, weight)


def code_onehot(code_block):
    return (code_block[:, :, None] == jnp.arange(K, dtype=jnp.int32)[None, None, :]).astype(
        jnp.float32
    )


def fetched_terms(queries, vectors, code_rows, codebook):
    query_count = queries.shape[0]
    exact_score = jnp.einsum("qcd,qd->qc", vectors, queries, precision=lax.Precision.HIGHEST)
    query_parts = queries.reshape(query_count, M, SUB)
    lookup = jnp.einsum(
        "qmj,kmj->qmk", query_parts, codebook.reshape(K, M, SUB), precision=lax.Precision.HIGHEST
    )

    def student_one(pieces):
        code_one, lookup_one = pieces
        return jnp.einsum(
            "cmk,mk->c", code_onehot(code_one), lookup_one, precision=lax.Precision.HIGHEST
        )

    student = lax.map(student_one, (code_rows, lookup))
    query_loss, weight = distill(exact_score, student)

    def table_one(pieces):
        code_one, weight_one = pieces
        return jnp.einsum(
            "cmk,c->mk", code_onehot(code_one), weight_one, precision=lax.Precision.HIGHEST
        )

    weight_table = lax.map(table_one, (code_rows, weight))
    gradient = jnp.einsum(
        "qmk,qmj->kmj", weight_table, query_parts, precision=lax.Precision.HIGHEST
    )
    return (query_loss, gradient.reshape(K, D))


def shards_any(queries, documents, doc_codes, codebook, candidate_owner, candidate_local):
    groups = lax.axis_size("grp")
    owners = lax.axis_size("dev")
    query_count = queries.shape[0]
    capacity = min(query_count, max(2, 2 * query_count * C // (groups * owners)))
    slot_count = groups * owners * capacity
    positions = slot_positions(candidate_owner, capacity)
    wanted = jnp.zeros((slot_count,), jnp.int32).at[positions].set(candidate_local.reshape(-1))
    asked = lax.all_to_all(
        lax.all_to_all(
            wanted.reshape(groups, owners, capacity), "grp", split_axis=0, concat_axis=0, tiled=True
        ),
        "dev",
        split_axis=1,
        concat_axis=1,
        tiled=True,
    )
    doc_index = asked.reshape(slot_count)
    found_rows = documents[doc_index].reshape(groups, owners, capacity, D)
    found_codes = doc_codes[doc_index].astype(jnp.float32).reshape(groups, owners, capacity, M)
    fetched, fetched_codes = (
        lax.all_to_all(
            lax.all_to_all(found_rows, "grp", split_axis=0, concat_axis=0, tiled=True),
            "dev",
            split_axis=1,
            concat_axis=1,
            tiled=True,
        ),
        lax.all_to_all(
            lax.all_to_all(found_codes, "grp", split_axis=0, concat_axis=0, tiled=True),
            "dev",
            split_axis=1,
            concat_axis=1,
            tiled=True,
        ),
    )
    vectors = fetched.reshape(slot_count, D)[positions].reshape(query_count, C, D)
    code_rows = (
        fetched_codes.reshape(slot_count, M)[positions].astype(jnp.int32).reshape(query_count, C, M)
    )
    query_loss, local_gradient = fetched_terms(queries, vectors, code_rows, codebook)
    partial_sum = lax.psum_scatter(local_gradient, "dev", scatter_dimension=0, tiled=True)
    codebook_gradient = lax.psum_scatter(partial_sum, "grp", scatter_dimension=1, tiled=True)
    return (codebook_gradient, query_loss)


def solution(mesh):
    in_specs = (
        P(("grp", "dev"), None),
        P(("grp", "dev"), None),
        P(("grp", "dev"), None),
        P(),
        P(("grp", "dev"), None),
        P(("grp", "dev"), None),
    )
    out_specs = (P("dev", "grp"), P(("grp", "dev")))

    def shards(queries, documents, *rest):
        once = dict(mesh.shape) == {"grp": 2, "dev": 16}
        once = once and queries.shape == (QN, D) and documents.shape == (LANE, D)
        return (shards_once if once else shards_any)(queries, documents, *rest)

    return jax.shard_map(shards, mesh=mesh, in_specs=in_specs, out_specs=out_specs, check_vma=False)
```

```python
import functools

import jax
import jax.numpy as jnp
from jax import lax
from jax.experimental import pallas as pl
from jax.experimental.pallas import tpu as pltpu
from jax.sharding import PartitionSpec as P

D = 1024
M = 128
K = 256
C = 32
SUB = 8

LANE = 128
TILES = D // LANE
SPT = LANE // SUB
QN = 4
HALF = TILES // 2
BLOCK = 16
TOGETHER = 4
ROWS = HALF * QN + SPT + 1


def iota(shape, axis):
    return lax.broadcasted_iota(jnp.int32, shape, axis)


def place():
    return lax.axis_index("grp"), lax.axis_index("dev")


def fetch(pairs, sems):
    copies = [pltpu.make_async_copy(src, dst, sems.at[i]) for i, (src, dst) in enumerate(pairs)]
    for copy in copies:
        copy.start()
    for copy in copies:
        copy.wait()


def thirds(value):
    first = value.astype(jnp.bfloat16)
    rest = value - first.astype(jnp.float32)
    second = rest.astype(jnp.bfloat16)
    return first, second, (rest - second.astype(jnp.float32)).astype(jnp.bfloat16)


def dot(a, b):
    return jnp.dot(a, b, preferred_element_type=jnp.float32)


def pack_kernel(*refs):
    q_ref, codes_ref, owner_ref, local_ref = refs[5:9]
    out_ref, codes_t, sems = refs[4], refs[9], refs[10]
    fetch(list(zip(refs[:4], refs[5:9])), sems)
    codes_t[...] = codes_ref[...].astype(jnp.float32).T
    owner, local = owner_ref[...], local_ref[...]
    diagonal = iota((C, C), 0) == iota((C, C), 1)
    row = jnp.zeros((1, LANE), jnp.float32)
    for q in range(QN):
        owner_col = jnp.sum(jnp.where(diagonal, owner[q : q + 1, :], 0), axis=1, keepdims=True)
        local_col = jnp.sum(jnp.where(diagonal, local[q : q + 1, :], 0), axis=1, keepdims=True)
        hit = owner_col + q * C == iota((C, LANE), 1)
        row += jnp.sum(
            jnp.where(hit, local_col.astype(jnp.float32), 0.0), axis=0, keepdims=True
        )
    for p in range(C):
        tile, core = (p // 16) * 4 + p % 4, p % 2
        base = p * ROWS
        for i in range(HALF):
            t = 2 * i + core
            out_ref[base + i * QN : base + (i + 1) * QN, :] = q_ref[:, t * LANE : (t + 1) * LANE]
        first = base + HALF * QN
        out_ref[first : first + SPT, :] = codes_t[tile * SPT : (tile + 1) * SPT, :]
        out_ref[first + SPT : first + SPT + 1, :] = row


def owner_kernel(codes_ref, other_ref, book_ref, docs_ref, other_docs_ref, out_ref, book_t, codes_t):
    core = lax.rem(lax.axis_index("dev"), 2)

    def put(i, column, value):
        for level, part in enumerate(thirds(value)):
            out_ref[level, i * LANE : (i + 1) * LANE, column * LANE : (column + 1) * LANE] = part

    for block, ref in enumerate((codes_ref, other_ref)):
        codes_t[block * M : (block + 1) * M, :] = ref[...].T
    for i in range(HALF):
        t = 2 * i + core
        columns = pl.ds(pl.multiple_of(t * LANE, LANE), LANE)
        for block, ref in enumerate((docs_ref, other_docs_ref)):
            put(i, block, ref[:, columns].T)
        book_t[0] = book_ref[:LANE, columns].T
        book_t[1] = book_ref[LANE:, columns].T
        for block in range(2):
            first = pl.multiple_of(block * M + t * SPT, SPT)
            rows = codes_t[pl.ds(first, SPT), :]
            made = []
            for m in range(SPT):
                code = jnp.broadcast_to(rows[m : m + 1, :], (SUB, LANE))
                index = lax.bitwise_and(code, LANE - 1)
                low = jnp.take_along_axis(book_t[0, m * SUB : (m + 1) * SUB, :], index, axis=1)
                high = jnp.take_along_axis(book_t[1, m * SUB : (m + 1) * SUB, :], index, axis=1)
                made.append(jnp.where(code >= LANE, high, low))
            put(i, 2 + block, jnp.concatenate(made, axis=0))


def query_rows(got_ref, row):
    return jnp.concatenate([got_ref[pl.ds(row + q, C, stride=ROWS), :] for q in range(QN)], axis=0)


def score_kernel(got_ref, table_ref, out_ref):
    group, dev = place()
    me = group * 16 + dev
    core = lax.rem(dev, 2)
    query = jnp.concatenate([query_rows(got_ref, i * QN) for i in range(HALF)], axis=1)
    q0, q1, q2 = thirds(query)
    t0, t1, t2 = table_ref[0], table_ref[1], table_ref[2]
    scores = dot(q0, t2) + dot(q2, t0) + dot(q1, t1)
    scores = scores + (dot(q0, t1) + dot(q1, t0))
    scores = scores + dot(q0, t0)
    asked = got_ref[pl.ds(ROWS - 1, C, stride=ROWS), :]
    lanes = iota((C, LANE), 1)
    wide = iota((LANE, LANE), 1)
    diagonal = iota((LANE, LANE), 0) == wide
    rows = []
    for block in range(2):
        owner = me if block == 0 else me + 1 - 2 * core
        local = jnp.concatenate(
            [
                jnp.sum(jnp.where(lanes == q * C + owner, asked, 0.0), axis=1, keepdims=True)
                for q in range(QN)
            ],
            axis=0,
        ).astype(jnp.int32)
        hit = wide == local
        for kind in range(2):
            first = (kind * 2 + block) * LANE
            column = jnp.sum(
                jnp.where(hit, scores[:, first : first + LANE], 0.0), axis=1, keepdims=True
            )
            rows.append(jnp.sum(jnp.where(diagonal, column, 0.0), axis=0, keepdims=True))
    mine = jnp.concatenate(rows, axis=0)
    for p in range(C):
        out_ref[p] = mine


def pair_kernel(got_ref, other_ref, out_ref, query_ref):
    group, dev = place()
    core, half = lax.rem(dev, 2), group * 2 + lax.div(lax.rem(dev, 4), 2)
    asked = got_ref[pl.ds(ROWS - 1, C, stride=ROWS), :]
    asked = jnp.concatenate([asked, jnp.zeros((LANE - C, LANE), jnp.float32)], axis=0).T
    local = jnp.concatenate([asked[q * C : (q + 1) * C, :C] for q in range(QN)], axis=1)
    local = local.astype(jnp.int32)
    for ref, tile in ((got_ref, core), (other_ref, 1 - core)):
        first, second, _ = thirds(query_rows(ref, half * QN))
        for rows in (slice(0, LANE), slice(LANE, 2 * LANE)):
            query_ref[tile, rows, :LANE] = first
            query_ref[tile, rows, LANE:] = second
        for o in range(C):
            index = jnp.broadcast_to(local[o : o + 1, :], (SUB, LANE))
            for part in range(SPT // SUB):
                row = o * ROWS + HALF * QN + part * SUB
                found = jnp.take_along_axis(ref[row : row + SUB, :], index, axis=1)
                at = pl.ds(pl.multiple_of(tile * SPT + part * SUB, SUB), SUB)
                out_ref[o, at, :] = found


def log_parts(scores):
    top = jnp.max(scores, axis=0, keepdims=True)
    shifted = scores - top
    powers = jnp.exp(shifted)
    total = jnp.sum(powers, axis=0, keepdims=True)
    return powers / total, shifted - jnp.log(total)


def block(first, weight, pairs_ref, query_ref, table, out_ref):
    words = [
        (iota((SUB, LANE), 0) + (first + v * SUB)).astype(jnp.float32) for v in range(BLOCK // SUB)
    ]

    @pl.loop(0, 2 * SPT // TOGETHER)
    def _(step):
        total = [[jnp.zeros((SUB, LANE), jnp.float32)] * len(words) for _ in range(TOGETHER)]
        for o in range(C):
            part = weight[o]
            for i in range(TOGETHER):
                row = pairs_ref[o, pl.ds(step * TOGETHER + i, 1), :]
                code = jnp.broadcast_to(row, (SUB, LANE))
                for v, word in enumerate(words):
                    total[i][v] += jnp.where(code == word, part, 0.0)
        rows = pl.ds(pl.multiple_of(step * (TOGETHER * BLOCK), TOGETHER * BLOCK), TOGETHER * BLOCK)
        first, second, _ = thirds(jnp.concatenate(sum(total, []), axis=0))
        table[rows, :LANE] = first
        table[rows, LANE:] = second

    subspace = lax.div(iota((BLOCK, LANE), 1), SUB)
    for tile in range(2):
        base = tile * SPT * BLOCK
        product = dot(table[base : base + SPT * BLOCK, :], query_ref[tile])
        product = product[:, :LANE] + product[:, LANE:]
        result = jnp.zeros((BLOCK, LANE), jnp.float32)
        for m in range(SPT):
            rows = product[m * BLOCK : (m + 1) * BLOCK, :]
            result += jnp.where(subspace == m, rows, 0.0)
        out_ref[:, tile * LANE : (tile + 1) * LANE] = result


def there_kernel(scores_ref, pairs_ref, query_ref, out_ref, weight_ref, loss_ref, table):
    group, dev = place()
    me = group * 16 + dev
    odd = lax.rem(iota((C, LANE), 0), 2) == 1

    def joined(mine, other):
        swapped = jnp.where(odd, pltpu.roll(other, 1, 0), pltpu.roll(other, C - 1, 0))
        return mine + swapped

    exact = joined(scores_ref[:, 0, :], scores_ref[:, 2, :])
    student = joined(scores_ref[:, 1, :], scores_ref[:, 3, :])
    teacher, log_teacher = log_parts(exact)
    soft, log_soft = log_parts(student)
    loss = jnp.sum(teacher * (log_teacher - log_soft), axis=0, keepdims=True)
    lanes = iota((1, LANE), 1)
    for q in range(QN):
        loss_ref[q] = jnp.sum(jnp.where(lanes == q * C + me, loss, 0.0))
    share = soft - teacher
    for o in range(C):
        weight_ref[o] = jnp.broadcast_to(share[o : o + 1, :], (SUB, LANE))
    block((dev ^ 2) * BLOCK, weight_ref, pairs_ref, query_ref, table, out_ref)


def here_kernel(weight_ref, pairs_ref, query_ref, out_ref, table):
    block(lax.axis_index("dev") * BLOCK, weight_ref, pairs_ref, query_ref, table, out_ref)


def vmem(n):
    return [pl.BlockSpec(memory_space=pltpu.VMEM)] * n


def call(kernel, outs, n_in, scratch=(), out_specs=None, flops=0, moved=0, space=pltpu.VMEM, mib=8):
    return pl.pallas_call(
        kernel,
        out_shape=outs,
        in_specs=[pl.BlockSpec(memory_space=space)] * n_in,
        out_specs=out_specs,
        scratch_shapes=list(scratch),
        compiler_params=pltpu.CompilerParams(vmem_limit_bytes=mib * 1024 * 1024),
        cost_estimate=pl.CostEstimate(flops=flops, bytes_accessed=moved, transcendentals=0),
    )


def f32(*shape):
    return jax.ShapeDtypeStruct(shape, jnp.float32)


def by_xor(value, bits, count):
    return lax.ppermute(value, "dev", [(i, i ^ bits) for i in range(count)])


def shards_once(queries, documents, doc_codes, codebook, candidate_owner, candidate_local):
    owners = lax.axis_size("dev")
    everyone = ("grp", "dev")
    other_docs = by_xor(documents, 1, owners)
    other_codes = by_xor(doc_codes, 1, owners)
    sent = call(
        pack_kernel,
        f32(C * ROWS, LANE),
        4,
        [
            pltpu.VMEM((QN, D), jnp.float32),
            pltpu.VMEM((LANE, M), jnp.int32),
            pltpu.VMEM((QN, C), jnp.int32),
            pltpu.VMEM((QN, C), jnp.int32),
            pltpu.VMEM((M, LANE), jnp.float32),
            pltpu.SemaphoreType.DMA((4,)),
        ],
        vmem(1)[0],
        0,
        1 << 20,
        pl.ANY,
        62,
    )(queries, doc_codes, candidate_owner, candidate_local)
    got = lax.all_to_all(
        sent.reshape(C, ROWS, 1, LANE), everyone, split_axis=0, concat_axis=0, tiled=True
    ).reshape(C * ROWS, LANE)
    table = call(
        owner_kernel,
        jax.ShapeDtypeStruct((3, HALF * LANE, 4 * LANE), jnp.bfloat16),
        5,
        [pltpu.VMEM((2, LANE, LANE), jnp.float32), pltpu.VMEM((2 * M, LANE), jnp.int32)],
        vmem(1)[0],
        1 << 22,
        1 << 21,
    )(doc_codes, other_codes, codebook, documents, other_docs)
    scores = call(score_kernel, f32(C, 4, LANE), 2, (), vmem(1)[0], 1 << 27, 1 << 21)(got, table)
    scores, after = lax.optimization_barrier((scores, got))
    all_scores = lax.all_to_all(scores, everyone, split_axis=0, concat_axis=0, tiled=True)
    pairs, columns = call(
        pair_kernel,
        (f32(C, 2 * SPT, LANE), jax.ShapeDtypeStruct((2, 2 * LANE, 2 * LANE), jnp.bfloat16)),
        2,
        (),
        tuple(vmem(2)),
        1 << 20,
        1 << 20,
    )(after, by_xor(after, 1, owners))
    built = [pltpu.VMEM((2 * SPT * BLOCK, 2 * LANE), jnp.bfloat16)]
    there, weight, query_loss = call(
        there_kernel,
        (f32(BLOCK, 2 * LANE), f32(C, SUB, LANE), f32(QN)),
        3,
        built,
        tuple(vmem(2)) + (pl.BlockSpec(memory_space=pltpu.SMEM),),
        1 << 27,
        1 << 21,
    )(all_scores, pairs, columns)
    far = by_xor(there, 2, owners)
    here = call(here_kernel, f32(BLOCK, 2 * LANE), 3, built, vmem(1)[0], 1 << 27, 1 << 21)(
        weight, pairs, columns
    )
    second = lax.rem(lax.div(lax.axis_index("dev"), 2), 2) == 1
    gradient = jnp.where(
        second, jnp.concatenate([far, here], 1), jnp.concatenate([here, far], 1)
    )
    return gradient, query_loss


def slot_positions(candidate_owner, capacity):
    owner_flat = candidate_owner.reshape(-1)
    ordinal = jnp.arange(owner_flat.shape[0], dtype=jnp.int32)
    earlier = (owner_flat[None, :] == owner_flat[:, None]) & (ordinal[None, :] < ordinal[:, None])
    rank_inside = jnp.sum(earlier.astype(jnp.int32), axis=1)
    return owner_flat * capacity + rank_inside


def distill(exact_score, student):
    teacher = jax.nn.softmax(exact_score, axis=-1)
    query_loss = jnp.sum(
        teacher * (jax.nn.log_softmax(exact_score, axis=-1) - jax.nn.log_softmax(student, axis=-1)),
        axis=-1,
    )
    weight = jax.nn.softmax(student, axis=-1) - teacher
    return (query_loss, weight)


def code_onehot(code_block):
    return (code_block[:, :, None] == jnp.arange(K, dtype=jnp.int32)[None, None, :]).astype(
        jnp.float32
    )


def fetched_terms(queries, vectors, code_rows, codebook):
    query_count = queries.shape[0]
    exact_score = jnp.einsum("qcd,qd->qc", vectors, queries, precision=lax.Precision.HIGHEST)
    query_parts = queries.reshape(query_count, M, SUB)
    lookup = jnp.einsum(
        "qmj,kmj->qmk", query_parts, codebook.reshape(K, M, SUB), precision=lax.Precision.HIGHEST
    )

    def student_one(pieces):
        code_one, lookup_one = pieces
        return jnp.einsum(
            "cmk,mk->c", code_onehot(code_one), lookup_one, precision=lax.Precision.HIGHEST
        )

    student = lax.map(student_one, (code_rows, lookup))
    query_loss, weight = distill(exact_score, student)

    def table_one(pieces):
        code_one, weight_one = pieces
        return jnp.einsum(
            "cmk,c->mk", code_onehot(code_one), weight_one, precision=lax.Precision.HIGHEST
        )

    weight_table = lax.map(table_one, (code_rows, weight))
    gradient = jnp.einsum(
        "qmk,qmj->kmj", weight_table, query_parts, precision=lax.Precision.HIGHEST
    )
    return (query_loss, gradient.reshape(K, D))


def shards_any(queries, documents, doc_codes, codebook, candidate_owner, candidate_local):
    groups = lax.axis_size("grp")
    owners = lax.axis_size("dev")
    query_count = queries.shape[0]
    capacity = min(query_count, max(2, 2 * query_count * C // (groups * owners)))
    slot_count = groups * owners * capacity
    positions = slot_positions(candidate_owner, capacity)
    wanted = jnp.zeros((slot_count,), jnp.int32).at[positions].set(candidate_local.reshape(-1))
    asked = lax.all_to_all(
        lax.all_to_all(
            wanted.reshape(groups, owners, capacity), "grp", split_axis=0, concat_axis=0, tiled=True
        ),
        "dev",
        split_axis=1,
        concat_axis=1,
        tiled=True,
    )
    doc_index = asked.reshape(slot_count)
    found_rows = documents[doc_index].reshape(groups, owners, capacity, D)
    found_codes = doc_codes[doc_index].astype(jnp.float32).reshape(groups, owners, capacity, M)
    fetched, fetched_codes = (
        lax.all_to_all(
            lax.all_to_all(found_rows, "grp", split_axis=0, concat_axis=0, tiled=True),
            "dev",
            split_axis=1,
            concat_axis=1,
            tiled=True,
        ),
        lax.all_to_all(
            lax.all_to_all(found_codes, "grp", split_axis=0, concat_axis=0, tiled=True),
            "dev",
            split_axis=1,
            concat_axis=1,
            tiled=True,
        ),
    )
    vectors = fetched.reshape(slot_count, D)[positions].reshape(query_count, C, D)
    code_rows = (
        fetched_codes.reshape(slot_count, M)[positions].astype(jnp.int32).reshape(query_count, C, M)
    )
    query_loss, local_gradient = fetched_terms(queries, vectors, code_rows, codebook)
    partial_sum = lax.psum_scatter(local_gradient, "dev", scatter_dimension=0, tiled=True)
    codebook_gradient = lax.psum_scatter(partial_sum, "grp", scatter_dimension=1, tiled=True)
    return (codebook_gradient, query_loss)


def solution(mesh):
    in_specs = (
        P(("grp", "dev"), None),
        P(("grp", "dev"), None),
        P(("grp", "dev"), None),
        P(),
        P(("grp", "dev"), None),
        P(("grp", "dev"), None),
    )
    out_specs = (P("dev", "grp"), P(("grp", "dev")))

    def shards(queries, documents, *rest):
        once = dict(mesh.shape) == {"grp": 2, "dev": 16}
        once = once and queries.shape == (QN, D) and documents.shape == (LANE, D)
        return (shards_once if once else shards_any)(queries, documents, *rest)

    return jax.shard_map(shards, mesh=mesh, in_specs=in_specs, out_specs=out_specs, check_vma=False)
```

```python
import functools

import jax
import jax.numpy as jnp
from jax import lax
from jax.experimental import pallas as pl
from jax.experimental.pallas import tpu as pltpu
from jax.sharding import PartitionSpec as P

D = 1024
M = 128
K = 256
C = 32
SUB = 8

LANE = 128
TILES = D // LANE
SPT = LANE // SUB
QN = 4
HALF = TILES // 2
BLOCK = 16
TOGETHER = 4
ROWS = HALF * QN + SUB + 1


def iota(shape, axis):
    return lax.broadcasted_iota(jnp.int32, shape, axis)


def place():
    return lax.axis_index("grp"), lax.axis_index("dev")


def fetch(pairs, sems):
    copies = [pltpu.make_async_copy(src, dst, sems.at[i]) for i, (src, dst) in enumerate(pairs)]
    for copy in copies:
        copy.start()
    for copy in copies:
        copy.wait()


def thirds(value):
    first = value.astype(jnp.bfloat16)
    rest = value - first.astype(jnp.float32)
    second = rest.astype(jnp.bfloat16)
    return first, second, (rest - second.astype(jnp.float32)).astype(jnp.bfloat16)


def dot(a, b):
    return jnp.dot(a, b, preferred_element_type=jnp.float32)


def pack_kernel(*refs):
    q_ref, codes_ref, owner_ref, local_ref = refs[5:9]
    out_ref, codes_t, sems = refs[4], refs[9], refs[10]
    fetch(list(zip(refs[:4], refs[5:9])), sems)
    codes_t[...] = codes_ref[...].astype(jnp.float32).T
    owner, local = owner_ref[...], local_ref[...]
    diagonal = iota((C, C), 0) == iota((C, C), 1)
    row = jnp.zeros((1, LANE), jnp.float32)
    for q in range(QN):
        owner_col = jnp.sum(jnp.where(diagonal, owner[q : q + 1, :], 0), axis=1, keepdims=True)
        local_col = jnp.sum(jnp.where(diagonal, local[q : q + 1, :], 0), axis=1, keepdims=True)
        hit = owner_col + q * C == iota((C, LANE), 1)
        row += jnp.sum(
            jnp.where(hit, local_col.astype(jnp.float32), 0.0), axis=0, keepdims=True
        )
    for p in range(C):
        tile, core = (p // 16) * 4 + p % 4, p % 2
        base = p * ROWS
        for i in range(HALF):
            t = 2 * i + core
            out_ref[base + i * QN : base + (i + 1) * QN, :] = q_ref[:, t * LANE : (t + 1) * LANE]
        first = base + HALF * QN
        start = tile * SPT + p // 4 % 2 * SUB
        out_ref[first : first + SUB, :] = codes_t[start : start + SUB, :]
        out_ref[first + SUB : first + SUB + 1, :] = row


def owner_kernel(codes_ref, other_ref, book_ref, docs_ref, other_docs_ref, out_ref, book_t, codes_t):
    core = lax.rem(lax.axis_index("dev"), 2)

    def put(i, column, value):
        for level, part in enumerate(thirds(value)):
            out_ref[level, i * LANE : (i + 1) * LANE, column * LANE : (column + 1) * LANE] = part

    for block, ref in enumerate((codes_ref, other_ref)):
        codes_t[block * M : (block + 1) * M, :] = ref[...].T
    for i in range(HALF):
        t = 2 * i + core
        columns = pl.ds(pl.multiple_of(t * LANE, LANE), LANE)
        for block, ref in enumerate((docs_ref, other_docs_ref)):
            put(i, block, ref[:, columns].T)
        book_t[0] = book_ref[:LANE, columns].T
        book_t[1] = book_ref[LANE:, columns].T
        for block in range(2):
            first = pl.multiple_of(block * M + t * SPT, SPT)
            rows = codes_t[pl.ds(first, SPT), :]
            made = []
            for m in range(SPT):
                code = jnp.broadcast_to(rows[m : m + 1, :], (SUB, LANE))
                index = lax.bitwise_and(code, LANE - 1)
                low = jnp.take_along_axis(book_t[0, m * SUB : (m + 1) * SUB, :], index, axis=1)
                high = jnp.take_along_axis(book_t[1, m * SUB : (m + 1) * SUB, :], index, axis=1)
                made.append(jnp.where(code >= LANE, high, low))
            put(i, 2 + block, jnp.concatenate(made, axis=0))


def query_rows(got_ref, row):
    return jnp.concatenate([got_ref[pl.ds(row + q, C, stride=ROWS), :] for q in range(QN)], axis=0)


def score_kernel(got_ref, table_ref, out_ref, codes_ref):
    group, dev = place()
    me = group * 16 + dev
    core = lax.rem(dev, 2)
    query = jnp.concatenate([query_rows(got_ref, i * QN) for i in range(HALF)], axis=1)
    q0, q1, q2 = thirds(query)
    t0, t1, t2 = table_ref[0], table_ref[1], table_ref[2]
    by_first = dot(jnp.concatenate([q0, q1, q2], axis=0), t0)
    by_second = dot(jnp.concatenate([q0, q1], axis=0), t1)
    scores = dot(q0, t2) + by_first[2 * LANE :] + by_second[LANE:]
    scores = scores + (by_second[:LANE] + by_first[LANE : 2 * LANE])
    scores = scores + by_first[:LANE]
    asked = got_ref[pl.ds(ROWS - 1, C, stride=ROWS), :]
    lanes = iota((C, LANE), 1)
    wide = iota((LANE, LANE), 1)
    diagonal = iota((LANE, LANE), 0) == wide
    rows = []
    for block in range(2):
        owner = me if block == 0 else me + 1 - 2 * core
        local = jnp.concatenate(
            [
                jnp.sum(jnp.where(lanes == q * C + owner, asked, 0.0), axis=1, keepdims=True)
                for q in range(QN)
            ],
            axis=0,
        ).astype(jnp.int32)
        hit = wide == local
        for kind in range(2):
            first = (kind * 2 + block) * LANE
            column = jnp.sum(
                jnp.where(hit, scores[:, first : first + LANE], 0.0), axis=1, keepdims=True
            )
            rows.append(jnp.sum(jnp.where(diagonal, column, 0.0), axis=0, keepdims=True))
    mine = jnp.concatenate(rows, axis=0)
    for p in range(C):
        out_ref[p] = mine
        first = p * ROWS + HALF * QN
        codes_ref[p] = got_ref[first : first + SUB, :]


def pair_kernel(got_ref, codes_ref, more_ref, other_ref, other_more_ref, out_ref, query_ref):
    group, dev = place()
    core, half = lax.rem(dev, 2), group * 2 + lax.div(lax.rem(dev, 4), 2)
    own = lax.rem(lax.div(dev, 4), 2)
    asked = got_ref[pl.ds(ROWS - 1, C, stride=ROWS), :]
    asked = jnp.concatenate([asked, jnp.zeros((LANE - C, LANE), jnp.float32)], axis=0).T
    local = jnp.concatenate([asked[q * C : (q + 1) * C, :C] for q in range(QN)], axis=1)
    local = local.astype(jnp.int32)
    for ref, tile in ((got_ref, core), (other_ref, 1 - core)):
        first, second, _ = thirds(query_rows(ref, half * QN))
        for rows in (slice(0, LANE), slice(LANE, 2 * LANE)):
            query_ref[tile, rows, :LANE] = first
            query_ref[tile, rows, LANE:] = second
    at = [
        pl.ds(pl.multiple_of(tile * SPT + part * SUB, SUB), SUB)
        for tile in (core, 1 - core)
        for part in (own, 1 - own)
    ]
    for o in range(C):
        index = jnp.broadcast_to(local[o : o + 1, :], (SUB, LANE))
        row = o * ROWS + HALF * QN
        found = (codes_ref[o], more_ref[o], other_ref[row : row + SUB, :], other_more_ref[o])
        for rows, value in zip(at, found):
            out_ref[o, rows, :] = jnp.take_along_axis(value, index, axis=1)


def log_parts(scores):
    top = jnp.max(scores, axis=0, keepdims=True)
    shifted = scores - top
    powers = jnp.exp(shifted)
    total = jnp.sum(powers, axis=0, keepdims=True)
    return powers / total, shifted - jnp.log(total)


def block(first, weight, pairs_ref, query_ref, table, out_ref):
    words = [
        (iota((SUB, LANE), 0) + (first + v * SUB)).astype(jnp.float32) for v in range(BLOCK // SUB)
    ]

    @pl.loop(0, 2 * SPT // TOGETHER)
    def _(step):
        total = [[jnp.zeros((SUB, LANE), jnp.float32)] * len(words) for _ in range(TOGETHER)]
        for o in range(C):
            part = weight[o]
            for i in range(TOGETHER):
                row = pairs_ref[o, pl.ds(step * TOGETHER + i, 1), :]
                code = jnp.broadcast_to(row, (SUB, LANE))
                for v, word in enumerate(words):
                    total[i][v] += jnp.where(code == word, part, 0.0)
        rows = pl.ds(pl.multiple_of(step * (TOGETHER * BLOCK), TOGETHER * BLOCK), TOGETHER * BLOCK)
        first, second, _ = thirds(jnp.concatenate(sum(total, []), axis=0))
        table[rows, :LANE] = first
        table[rows, LANE:] = second

    subspace = lax.div(iota((BLOCK, LANE), 1), SUB)
    for tile in range(2):
        base = tile * SPT * BLOCK
        product = dot(table[base : base + SPT * BLOCK, :], query_ref[tile])
        product = product[:, :LANE] + product[:, LANE:]
        result = jnp.zeros((BLOCK, LANE), jnp.float32)
        for m in range(SPT):
            rows = product[m * BLOCK : (m + 1) * BLOCK, :]
            result += jnp.where(subspace == m, rows, 0.0)
        out_ref[:, tile * LANE : (tile + 1) * LANE] = result


def there_kernel(scores_ref, pairs_ref, query_ref, out_ref, weight_ref, loss_ref, table):
    dev = lax.axis_index("dev")
    odd = lax.rem(iota((C, LANE), 0), 2) == 1

    def joined(mine, other):
        swapped = jnp.where(odd, pltpu.roll(other, 1, 0), pltpu.roll(other, C - 1, 0))
        return mine + swapped

    exact = joined(scores_ref[:, 0, :], scores_ref[:, 2, :])
    student = joined(scores_ref[:, 1, :], scores_ref[:, 3, :])
    teacher, log_teacher = log_parts(exact)
    soft, log_soft = log_parts(student)
    loss = jnp.sum(teacher * (log_teacher - log_soft), axis=0, keepdims=True)
    loss_ref[...] = loss
    share = soft - teacher
    for o in range(C):
        weight_ref[o] = jnp.broadcast_to(share[o : o + 1, :], (SUB, LANE))
    block((dev ^ 2) * BLOCK, weight_ref, pairs_ref, query_ref, table, out_ref)


def here_kernel(weight_ref, loss_ref, pairs_ref, query_ref, out_ref, own_loss_ref, table):
    group, dev = place()
    lanes = iota((1, LANE), 1)
    for q in range(QN):
        mine = lanes == q * C + group * 16 + dev
        own_loss_ref[q] = jnp.sum(jnp.where(mine, loss_ref[...], 0.0))
    block(lax.axis_index("dev") * BLOCK, weight_ref, pairs_ref, query_ref, table, out_ref)


def vmem(n):
    return [pl.BlockSpec(memory_space=pltpu.VMEM)] * n


def call(kernel, outs, n_in, scratch=(), out_specs=None, flops=0, moved=0, space=pltpu.VMEM, mib=8):
    return pl.pallas_call(
        kernel,
        out_shape=outs,
        in_specs=[pl.BlockSpec(memory_space=space)] * n_in,
        out_specs=out_specs,
        scratch_shapes=list(scratch),
        compiler_params=pltpu.CompilerParams(vmem_limit_bytes=mib * 1024 * 1024),
        cost_estimate=pl.CostEstimate(flops=flops, bytes_accessed=moved, transcendentals=0),
    )


def f32(*shape):
    return jax.ShapeDtypeStruct(shape, jnp.float32)


def by_xor(value, bits, count):
    return lax.ppermute(value, "dev", [(i, i ^ bits) for i in range(count)])


def shards_once(queries, documents, doc_codes, codebook, candidate_owner, candidate_local):
    owners = lax.axis_size("dev")
    everyone = ("grp", "dev")
    other_docs = by_xor(documents, 1, owners)
    other_codes = by_xor(doc_codes, 1, owners)
    sent = call(
        pack_kernel,
        f32(C * ROWS, LANE),
        4,
        [
            pltpu.VMEM((QN, D), jnp.float32),
            pltpu.VMEM((LANE, M), jnp.int32),
            pltpu.VMEM((QN, C), jnp.int32),
            pltpu.VMEM((QN, C), jnp.int32),
            pltpu.VMEM((M, LANE), jnp.float32),
            pltpu.SemaphoreType.DMA((4,)),
        ],
        vmem(1)[0],
        0,
        1 << 20,
        pl.ANY,
        62,
    )(queries, doc_codes, candidate_owner, candidate_local)
    got = lax.all_to_all(
        sent.reshape(C, ROWS, 1, LANE), everyone, split_axis=0, concat_axis=0, tiled=True
    ).reshape(C * ROWS, LANE)
    table = call(
        owner_kernel,
        jax.ShapeDtypeStruct((3, HALF * LANE, 4 * LANE), jnp.bfloat16),
        5,
        [pltpu.VMEM((2, LANE, LANE), jnp.float32), pltpu.VMEM((2 * M, LANE), jnp.int32)],
        vmem(1)[0],
        1 << 22,
        1 << 21,
    )(doc_codes, other_codes, codebook, documents, other_docs)
    scores, codes = call(
        score_kernel, (f32(C, 4, LANE), f32(C, SUB, LANE)), 2, (), tuple(vmem(2)), 1 << 27, 1 << 21
    )(got, table)
    more = by_xor(codes, 4, owners)
    scores, after = lax.optimization_barrier((scores, got))
    all_scores = lax.all_to_all(scores, everyone, split_axis=0, concat_axis=0, tiled=True)
    pairs, columns = call(
        pair_kernel,
        (f32(C, 2 * SPT, LANE), jax.ShapeDtypeStruct((2, 2 * LANE, 2 * LANE), jnp.bfloat16)),
        5,
        (),
        tuple(vmem(2)),
        1 << 20,
        1 << 20,
    )(after, codes, more, by_xor(after, 1, owners), by_xor(codes, 5, owners))
    built = [pltpu.VMEM((2 * SPT * BLOCK, 2 * LANE), jnp.bfloat16)]
    there, weight, losses = call(
        there_kernel,
        (f32(BLOCK, 2 * LANE), f32(C, SUB, LANE), f32(1, LANE)),
        3,
        built,
        tuple(vmem(3)),
        1 << 27,
        1 << 21,
    )(all_scores, pairs, columns)
    far = by_xor(there, 2, owners)
    here, query_loss = call(
        here_kernel,
        (f32(BLOCK, 2 * LANE), f32(QN)),
        4,
        built,
        (vmem(1)[0], pl.BlockSpec(memory_space=pltpu.SMEM)),
        1 << 27,
        1 << 21,
    )(weight, losses, pairs, columns)
    second = lax.rem(lax.div(lax.axis_index("dev"), 2), 2) == 1
    gradient = jnp.where(
        second, jnp.concatenate([far, here], 1), jnp.concatenate([here, far], 1)
    )
    return gradient, query_loss


def slot_positions(candidate_owner, capacity):
    owner_flat = candidate_owner.reshape(-1)
    ordinal = jnp.arange(owner_flat.shape[0], dtype=jnp.int32)
    earlier = (owner_flat[None, :] == owner_flat[:, None]) & (ordinal[None, :] < ordinal[:, None])
    rank_inside = jnp.sum(earlier.astype(jnp.int32), axis=1)
    return owner_flat * capacity + rank_inside


def distill(exact_score, student):
    teacher = jax.nn.softmax(exact_score, axis=-1)
    query_loss = jnp.sum(
        teacher * (jax.nn.log_softmax(exact_score, axis=-1) - jax.nn.log_softmax(student, axis=-1)),
        axis=-1,
    )
    weight = jax.nn.softmax(student, axis=-1) - teacher
    return (query_loss, weight)


def code_onehot(code_block):
    return (code_block[:, :, None] == jnp.arange(K, dtype=jnp.int32)[None, None, :]).astype(
        jnp.float32
    )


def fetched_terms(queries, vectors, code_rows, codebook):
    query_count = queries.shape[0]
    exact_score = jnp.einsum("qcd,qd->qc", vectors, queries, precision=lax.Precision.HIGHEST)
    query_parts = queries.reshape(query_count, M, SUB)
    lookup = jnp.einsum(
        "qmj,kmj->qmk", query_parts, codebook.reshape(K, M, SUB), precision=lax.Precision.HIGHEST
    )

    def student_one(pieces):
        code_one, lookup_one = pieces
        return jnp.einsum(
            "cmk,mk->c", code_onehot(code_one), lookup_one, precision=lax.Precision.HIGHEST
        )

    student = lax.map(student_one, (code_rows, lookup))
    query_loss, weight = distill(exact_score, student)

    def table_one(pieces):
        code_one, weight_one = pieces
        return jnp.einsum(
            "cmk,c->mk", code_onehot(code_one), weight_one, precision=lax.Precision.HIGHEST
        )

    weight_table = lax.map(table_one, (code_rows, weight))
    gradient = jnp.einsum(
        "qmk,qmj->kmj", weight_table, query_parts, precision=lax.Precision.HIGHEST
    )
    return (query_loss, gradient.reshape(K, D))


def shards_any(queries, documents, doc_codes, codebook, candidate_owner, candidate_local):
    groups = lax.axis_size("grp")
    owners = lax.axis_size("dev")
    query_count = queries.shape[0]
    capacity = min(query_count, max(2, 2 * query_count * C // (groups * owners)))
    slot_count = groups * owners * capacity
    positions = slot_positions(candidate_owner, capacity)
    wanted = jnp.zeros((slot_count,), jnp.int32).at[positions].set(candidate_local.reshape(-1))
    asked = lax.all_to_all(
        lax.all_to_all(
            wanted.reshape(groups, owners, capacity), "grp", split_axis=0, concat_axis=0, tiled=True
        ),
        "dev",
        split_axis=1,
        concat_axis=1,
        tiled=True,
    )
    doc_index = asked.reshape(slot_count)
    found_rows = documents[doc_index].reshape(groups, owners, capacity, D)
    found_codes = doc_codes[doc_index].astype(jnp.float32).reshape(groups, owners, capacity, M)
    fetched, fetched_codes = (
        lax.all_to_all(
            lax.all_to_all(found_rows, "grp", split_axis=0, concat_axis=0, tiled=True),
            "dev",
            split_axis=1,
            concat_axis=1,
            tiled=True,
        ),
        lax.all_to_all(
            lax.all_to_all(found_codes, "grp", split_axis=0, concat_axis=0, tiled=True),
            "dev",
            split_axis=1,
            concat_axis=1,
            tiled=True,
        ),
    )
    vectors = fetched.reshape(slot_count, D)[positions].reshape(query_count, C, D)
    code_rows = (
        fetched_codes.reshape(slot_count, M)[positions].astype(jnp.int32).reshape(query_count, C, M)
    )
    query_loss, local_gradient = fetched_terms(queries, vectors, code_rows, codebook)
    partial_sum = lax.psum_scatter(local_gradient, "dev", scatter_dimension=0, tiled=True)
    codebook_gradient = lax.psum_scatter(partial_sum, "grp", scatter_dimension=1, tiled=True)
    return (codebook_gradient, query_loss)


def solution(mesh):
    in_specs = (
        P(("grp", "dev"), None),
        P(("grp", "dev"), None),
        P(("grp", "dev"), None),
        P(),
        P(("grp", "dev"), None),
        P(("grp", "dev"), None),
    )
    out_specs = (P("dev", "grp"), P(("grp", "dev")))

    def shards(queries, documents, *rest):
        once = dict(mesh.shape) == {"grp": 2, "dev": 16}
        once = once and queries.shape == (QN, D) and documents.shape == (LANE, D)
        return (shards_once if once else shards_any)(queries, documents, *rest)

    return jax.shard_map(shards, mesh=mesh, in_specs=in_specs, out_specs=out_specs, check_vma=False)
```

```python
import functools

import jax
import jax.numpy as jnp
from jax import lax
from jax.experimental import pallas as pl
from jax.experimental.pallas import tpu as pltpu
from jax.sharding import PartitionSpec as P

D = 1024
M = 128
K = 256
C = 32
SUB = 8

LANE = 128
TILES = D // LANE
SPT = LANE // SUB
QN = 4
HALF = TILES // 2
BLOCK = 16
TOGETHER = 16
ROWS = HALF * QN + SUB + 1


def iota(shape, axis):
    return lax.broadcasted_iota(jnp.int32, shape, axis)


def place():
    return lax.axis_index("grp"), lax.axis_index("dev")


def fetch(pairs, sems):
    copies = [pltpu.make_async_copy(src, dst, sems.at[i]) for i, (src, dst) in enumerate(pairs)]
    for copy in copies:
        copy.start()
    for copy in copies:
        copy.wait()


def thirds(value):
    first = value.astype(jnp.bfloat16)
    rest = value - first.astype(jnp.float32)
    second = rest.astype(jnp.bfloat16)
    return first, second, (rest - second.astype(jnp.float32)).astype(jnp.bfloat16)


def dot(a, b):
    return jnp.dot(a, b, preferred_element_type=jnp.float32)


def pack_kernel(*refs):
    q_ref, codes_ref, owner_ref, local_ref = refs[5:9]
    out_ref, codes_t, sems = refs[4], refs[9], refs[10]
    fetch(list(zip(refs[:4], refs[5:9])), sems)
    codes_t[...] = codes_ref[...].astype(jnp.float32).T
    owner, local = owner_ref[...], local_ref[...]
    diagonal = iota((C, C), 0) == iota((C, C), 1)
    row = jnp.zeros((1, LANE), jnp.float32)
    for q in range(QN):
        owner_col = jnp.sum(jnp.where(diagonal, owner[q : q + 1, :], 0), axis=1, keepdims=True)
        local_col = jnp.sum(jnp.where(diagonal, local[q : q + 1, :], 0), axis=1, keepdims=True)
        hit = owner_col + q * C == iota((C, LANE), 1)
        row += jnp.sum(
            jnp.where(hit, local_col.astype(jnp.float32), 0.0), axis=0, keepdims=True
        )
    for p in range(C):
        tile, core = (p // 16) * 4 + p % 4, p % 2
        base = p * ROWS
        for i in range(HALF):
            t = 2 * i + core
            out_ref[base + i * QN : base + (i + 1) * QN, :] = q_ref[:, t * LANE : (t + 1) * LANE]
        first = base + HALF * QN
        start = tile * SPT + p // 4 % 2 * SUB
        out_ref[first : first + SUB, :] = codes_t[start : start + SUB, :]
        out_ref[first + SUB : first + SUB + 1, :] = row


def owner_kernel(codes_ref, other_ref, book_ref, docs_ref, other_docs_ref, out_ref, book_t, codes_t):
    core = lax.rem(lax.axis_index("dev"), 2)

    def put(i, column, value):
        for level, part in enumerate(thirds(value)):
            out_ref[level, i * LANE : (i + 1) * LANE, column * LANE : (column + 1) * LANE] = part

    for block, ref in enumerate((codes_ref, other_ref)):
        codes_t[block * M : (block + 1) * M, :] = ref[...].T
    for i in range(HALF):
        t = 2 * i + core
        columns = pl.ds(pl.multiple_of(t * LANE, LANE), LANE)
        for block, ref in enumerate((docs_ref, other_docs_ref)):
            put(i, block, ref[:, columns].T)
        book_t[0] = book_ref[:LANE, columns].T
        book_t[1] = book_ref[LANE:, columns].T
        for block in range(2):
            first = pl.multiple_of(block * M + t * SPT, SPT)
            rows = codes_t[pl.ds(first, SPT), :]
            made = []
            for m in range(SPT):
                code = jnp.broadcast_to(rows[m : m + 1, :], (SUB, LANE))
                index = lax.bitwise_and(code, LANE - 1)
                low = jnp.take_along_axis(book_t[0, m * SUB : (m + 1) * SUB, :], index, axis=1)
                high = jnp.take_along_axis(book_t[1, m * SUB : (m + 1) * SUB, :], index, axis=1)
                made.append(jnp.where(code >= LANE, high, low))
            put(i, 2 + block, jnp.concatenate(made, axis=0))


def query_rows(got_ref, row):
    return jnp.concatenate([got_ref[pl.ds(row + q, C, stride=ROWS), :] for q in range(QN)], axis=0)


def score_kernel(got_ref, table_ref, out_ref, codes_ref):
    group, dev = place()
    me = group * 16 + dev
    core = lax.rem(dev, 2)
    query = jnp.concatenate([query_rows(got_ref, i * QN) for i in range(HALF)], axis=1)
    q0, q1, q2 = thirds(query)
    t0, t1, t2 = table_ref[0], table_ref[1], table_ref[2]
    by_first = dot(jnp.concatenate([q0, q1, q2], axis=0), t0)
    by_second = dot(jnp.concatenate([q0, q1], axis=0), t1)
    scores = dot(q0, t2) + by_first[2 * LANE :] + by_second[LANE:]
    scores = scores + (by_second[:LANE] + by_first[LANE : 2 * LANE])
    scores = scores + by_first[:LANE]
    asked = got_ref[pl.ds(ROWS - 1, C, stride=ROWS), :]
    lanes = iota((C, LANE), 1)
    wide = iota((LANE, LANE), 1)
    diagonal = iota((LANE, LANE), 0) == wide
    rows = []
    for block in range(2):
        owner = me if block == 0 else me + 1 - 2 * core
        local = jnp.concatenate(
            [
                jnp.sum(jnp.where(lanes == q * C + owner, asked, 0.0), axis=1, keepdims=True)
                for q in range(QN)
            ],
            axis=0,
        ).astype(jnp.int32)
        hit = wide == local
        for kind in range(2):
            first = (kind * 2 + block) * LANE
            column = jnp.sum(
                jnp.where(hit, scores[:, first : first + LANE], 0.0), axis=1, keepdims=True
            )
            rows.append(jnp.sum(jnp.where(diagonal, column, 0.0), axis=0, keepdims=True))
    mine = jnp.concatenate(rows, axis=0)
    for p in range(C):
        out_ref[p] = mine
        first = p * ROWS + HALF * QN
        codes_ref[p] = got_ref[first : first + SUB, :]


def pair_kernel(got_ref, near_ref, z_ref, x_ref, both_ref, out_ref, query_ref):
    group, dev = place()
    across = lax.rem(lax.div(dev, 2), 2)
    own = lax.rem(lax.div(dev, 4), 2)
    asked = got_ref[pl.ds(ROWS - 1, C, stride=ROWS), :]
    asked = jnp.concatenate([asked, jnp.zeros((LANE - C, LANE), jnp.float32)], axis=0).T
    local = jnp.concatenate([asked[q * C : (q + 1) * C, :C] for q in range(QN)], axis=1)
    local = local.astype(jnp.int32)
    for tile in range(2):
        first, second, _ = thirds(query_rows(got_ref, (group * 2 + tile) * QN))
        for rows in (slice(0, LANE), slice(LANE, 2 * LANE)):
            query_ref[tile, rows, :LANE] = first
            query_ref[tile, rows, LANE:] = second
    at = [
        pl.ds(pl.multiple_of(tile * SPT + part * SUB, SUB), SUB)
        for tile in (across, 1 - across)
        for part in (own, 1 - own)
    ]
    for o in range(C):
        index = jnp.broadcast_to(local[o : o + 1, :], (SUB, LANE))
        for rows, ref in zip(at, (near_ref, z_ref, x_ref, both_ref)):
            out_ref[o, rows, :] = jnp.take_along_axis(ref[o], index, axis=1)


def log_parts(scores):
    top = jnp.max(scores, axis=0, keepdims=True)
    shifted = scores - top
    powers = jnp.exp(shifted)
    total = jnp.sum(powers, axis=0, keepdims=True)
    return powers / total, shifted - jnp.log(total)


def block(first, weight, pairs_ref, query_ref, table, out_ref):
    words = [
        (iota((SUB, LANE), 0) + (first + v * SUB)).astype(jnp.float32) for v in range(BLOCK // SUB)
    ]

    @pl.loop(0, 2 * SPT // TOGETHER)
    def _(step):
        total = [[jnp.zeros((SUB, LANE), jnp.float32)] * len(words) for _ in range(TOGETHER)]
        for o in range(C):
            part = weight[o]
            for i in range(TOGETHER):
                row = pairs_ref[o, pl.ds(step * TOGETHER + i, 1), :]
                code = jnp.broadcast_to(row, (SUB, LANE))
                for v, word in enumerate(words):
                    total[i][v] += jnp.where(code == word, part, 0.0)
        rows = pl.ds(pl.multiple_of(step * (TOGETHER * BLOCK), TOGETHER * BLOCK), TOGETHER * BLOCK)
        first, second, _ = thirds(jnp.concatenate(sum(total, []), axis=0))
        table[rows, :LANE] = first
        table[rows, LANE:] = second

    subspace = lax.div(iota((BLOCK, LANE), 1), SUB)
    for tile in range(2):
        base = tile * SPT * BLOCK
        product = dot(table[base : base + SPT * BLOCK, :], query_ref[tile])
        product = product[:, :LANE] + product[:, LANE:]
        result = jnp.zeros((BLOCK, LANE), jnp.float32)
        for m in range(SPT):
            rows = product[m * BLOCK : (m + 1) * BLOCK, :]
            result += jnp.where(subspace == m, rows, 0.0)
        out_ref[:, tile * LANE : (tile + 1) * LANE] = result


def there_kernel(scores_ref, pairs_ref, query_ref, out_ref, weight_ref, loss_ref, table):
    dev = lax.axis_index("dev")
    odd = lax.rem(iota((C, LANE), 0), 2) == 1

    def joined(mine, other):
        swapped = jnp.where(odd, pltpu.roll(other, 1, 0), pltpu.roll(other, C - 1, 0))
        return mine + swapped

    exact = joined(scores_ref[:, 0, :], scores_ref[:, 2, :])
    student = joined(scores_ref[:, 1, :], scores_ref[:, 3, :])
    teacher, log_teacher = log_parts(exact)
    soft, log_soft = log_parts(student)
    loss = jnp.sum(teacher * (log_teacher - log_soft), axis=0, keepdims=True)
    loss_ref[...] = loss
    share = soft - teacher
    for o in range(C):
        weight_ref[o] = jnp.broadcast_to(share[o : o + 1, :], (SUB, LANE))
    block((dev ^ 1) * BLOCK, weight_ref, pairs_ref, query_ref, table, out_ref)


def here_kernel(weight_ref, loss_ref, pairs_ref, query_ref, out_ref, own_loss_ref, table):
    group, dev = place()
    lanes = iota((1, LANE), 1)
    for q in range(QN):
        mine = lanes == q * C + group * 16 + dev
        own_loss_ref[q] = jnp.sum(jnp.where(mine, loss_ref[...], 0.0))
    block(lax.axis_index("dev") * BLOCK, weight_ref, pairs_ref, query_ref, table, out_ref)


def vmem(n):
    return [pl.BlockSpec(memory_space=pltpu.VMEM)] * n


def call(kernel, outs, n_in, scratch=(), out_specs=None, flops=0, moved=0, space=pltpu.VMEM, mib=8):
    return pl.pallas_call(
        kernel,
        out_shape=outs,
        in_specs=[pl.BlockSpec(memory_space=space)] * n_in,
        out_specs=out_specs,
        scratch_shapes=list(scratch),
        compiler_params=pltpu.CompilerParams(vmem_limit_bytes=mib * 1024 * 1024),
        cost_estimate=pl.CostEstimate(flops=flops, bytes_accessed=moved, transcendentals=0),
    )


def f32(*shape):
    return jax.ShapeDtypeStruct(shape, jnp.float32)


def by_xor(value, bits, count):
    return lax.ppermute(value, "dev", [(i, i ^ bits) for i in range(count)])


def shards_once(queries, documents, doc_codes, codebook, candidate_owner, candidate_local):
    owners = lax.axis_size("dev")
    everyone = ("grp", "dev")
    other_docs = by_xor(documents, 1, owners)
    other_codes = by_xor(doc_codes, 1, owners)
    sent = call(
        pack_kernel,
        f32(C * ROWS, LANE),
        4,
        [
            pltpu.VMEM((QN, D), jnp.float32),
            pltpu.VMEM((LANE, M), jnp.int32),
            pltpu.VMEM((QN, C), jnp.int32),
            pltpu.VMEM((QN, C), jnp.int32),
            pltpu.VMEM((M, LANE), jnp.float32),
            pltpu.SemaphoreType.DMA((4,)),
        ],
        vmem(1)[0],
        0,
        1 << 20,
        pl.ANY,
        62,
    )(queries, doc_codes, candidate_owner, candidate_local)
    got = lax.all_to_all(
        sent.reshape(C, ROWS, 1, LANE), everyone, split_axis=0, concat_axis=0, tiled=True
    ).reshape(C * ROWS, LANE)
    table = call(
        owner_kernel,
        jax.ShapeDtypeStruct((3, HALF * LANE, 4 * LANE), jnp.bfloat16),
        5,
        [pltpu.VMEM((2, LANE, LANE), jnp.float32), pltpu.VMEM((2 * M, LANE), jnp.int32)],
        vmem(1)[0],
        1 << 22,
        1 << 21,
    )(doc_codes, other_codes, codebook, documents, other_docs)
    scores, codes = call(
        score_kernel, (f32(C, 4, LANE), f32(C, SUB, LANE)), 2, (), tuple(vmem(2)), 1 << 27, 1 << 21
    )(got, table)
    all_scores = lax.all_to_all(scores, everyone, split_axis=0, concat_axis=0, tiled=True)
    pairs, columns = call(
        pair_kernel,
        (f32(C, 2 * SPT, LANE), jax.ShapeDtypeStruct((2, 2 * LANE, 2 * LANE), jnp.bfloat16)),
        5,
        (),
        tuple(vmem(2)),
        1 << 20,
        1 << 20,
    )(got, codes, *[by_xor(codes, bits, owners) for bits in (4, 2, 6)])
    built = [pltpu.VMEM((2 * SPT * BLOCK, 2 * LANE), jnp.bfloat16)]
    there, weight, losses = call(
        there_kernel,
        (f32(BLOCK, 2 * LANE), f32(C, SUB, LANE), f32(1, LANE)),
        3,
        built,
        tuple(vmem(3)),
        1 << 27,
        1 << 21,
    )(all_scores, pairs, columns)
    far = by_xor(there, 1, owners)
    here, query_loss = call(
        here_kernel,
        (f32(BLOCK, 2 * LANE), f32(QN)),
        4,
        built,
        (vmem(1)[0], pl.BlockSpec(memory_space=pltpu.SMEM)),
        1 << 27,
        1 << 21,
    )(weight, losses, pairs, columns)
    odd = lax.rem(lax.axis_index("dev"), 2) == 1
    even, later = jnp.where(odd, far, here), jnp.where(odd, here, far)
    gradient = jnp.concatenate(
        [even[:, :LANE], later[:, :LANE], even[:, LANE:], later[:, LANE:]], axis=1
    )
    return gradient, query_loss


def slot_positions(candidate_owner, capacity):
    owner_flat = candidate_owner.reshape(-1)
    ordinal = jnp.arange(owner_flat.shape[0], dtype=jnp.int32)
    earlier = (owner_flat[None, :] == owner_flat[:, None]) & (ordinal[None, :] < ordinal[:, None])
    rank_inside = jnp.sum(earlier.astype(jnp.int32), axis=1)
    return owner_flat * capacity + rank_inside


def distill(exact_score, student):
    teacher = jax.nn.softmax(exact_score, axis=-1)
    query_loss = jnp.sum(
        teacher * (jax.nn.log_softmax(exact_score, axis=-1) - jax.nn.log_softmax(student, axis=-1)),
        axis=-1,
    )
    weight = jax.nn.softmax(student, axis=-1) - teacher
    return (query_loss, weight)


def code_onehot(code_block):
    return (code_block[:, :, None] == jnp.arange(K, dtype=jnp.int32)[None, None, :]).astype(
        jnp.float32
    )


def fetched_terms(queries, vectors, code_rows, codebook):
    query_count = queries.shape[0]
    exact_score = jnp.einsum("qcd,qd->qc", vectors, queries, precision=lax.Precision.HIGHEST)
    query_parts = queries.reshape(query_count, M, SUB)
    lookup = jnp.einsum(
        "qmj,kmj->qmk", query_parts, codebook.reshape(K, M, SUB), precision=lax.Precision.HIGHEST
    )

    def student_one(pieces):
        code_one, lookup_one = pieces
        return jnp.einsum(
            "cmk,mk->c", code_onehot(code_one), lookup_one, precision=lax.Precision.HIGHEST
        )

    student = lax.map(student_one, (code_rows, lookup))
    query_loss, weight = distill(exact_score, student)

    def table_one(pieces):
        code_one, weight_one = pieces
        return jnp.einsum(
            "cmk,c->mk", code_onehot(code_one), weight_one, precision=lax.Precision.HIGHEST
        )

    weight_table = lax.map(table_one, (code_rows, weight))
    gradient = jnp.einsum(
        "qmk,qmj->kmj", weight_table, query_parts, precision=lax.Precision.HIGHEST
    )
    return (query_loss, gradient.reshape(K, D))


def shards_any(queries, documents, doc_codes, codebook, candidate_owner, candidate_local):
    groups = lax.axis_size("grp")
    owners = lax.axis_size("dev")
    query_count = queries.shape[0]
    capacity = min(query_count, max(2, 2 * query_count * C // (groups * owners)))
    slot_count = groups * owners * capacity
    positions = slot_positions(candidate_owner, capacity)
    wanted = jnp.zeros((slot_count,), jnp.int32).at[positions].set(candidate_local.reshape(-1))
    asked = lax.all_to_all(
        lax.all_to_all(
            wanted.reshape(groups, owners, capacity), "grp", split_axis=0, concat_axis=0, tiled=True
        ),
        "dev",
        split_axis=1,
        concat_axis=1,
        tiled=True,
    )
    doc_index = asked.reshape(slot_count)
    found_rows = documents[doc_index].reshape(groups, owners, capacity, D)
    found_codes = doc_codes[doc_index].astype(jnp.float32).reshape(groups, owners, capacity, M)
    fetched, fetched_codes = (
        lax.all_to_all(
            lax.all_to_all(found_rows, "grp", split_axis=0, concat_axis=0, tiled=True),
            "dev",
            split_axis=1,
            concat_axis=1,
            tiled=True,
        ),
        lax.all_to_all(
            lax.all_to_all(found_codes, "grp", split_axis=0, concat_axis=0, tiled=True),
            "dev",
            split_axis=1,
            concat_axis=1,
            tiled=True,
        ),
    )
    vectors = fetched.reshape(slot_count, D)[positions].reshape(query_count, C, D)
    code_rows = (
        fetched_codes.reshape(slot_count, M)[positions].astype(jnp.int32).reshape(query_count, C, M)
    )
    query_loss, local_gradient = fetched_terms(queries, vectors, code_rows, codebook)
    partial_sum = lax.psum_scatter(local_gradient, "dev", scatter_dimension=0, tiled=True)
    codebook_gradient = lax.psum_scatter(partial_sum, "grp", scatter_dimension=1, tiled=True)
    return (codebook_gradient, query_loss)


def solution(mesh):
    in_specs = (
        P(("grp", "dev"), None),
        P(("grp", "dev"), None),
        P(("grp", "dev"), None),
        P(),
        P(("grp", "dev"), None),
        P(("grp", "dev"), None),
    )
    out_specs = (P("dev", "grp"), P(("grp", "dev")))

    def shards(queries, documents, *rest):
        once = dict(mesh.shape) == {"grp": 2, "dev": 16}
        once = once and queries.shape == (QN, D) and documents.shape == (LANE, D)
        return (shards_once if once else shards_any)(queries, documents, *rest)

    return jax.shard_map(shards, mesh=mesh, in_specs=in_specs, out_specs=out_specs, check_vma=False)
```

```python
import functools

import jax
import jax.numpy as jnp
from jax import lax
from jax.experimental import pallas as pl
from jax.experimental.pallas import tpu as pltpu
from jax.sharding import PartitionSpec as P

D = 1024
M = 128
K = 256
C = 32
SUB = 8

LANE = 128
TILES = D // LANE
SPT = LANE // SUB
QN = 4
HALF = TILES // 2
BLOCK = 16
TOGETHER = 16
ROWS = HALF * QN + SUB + 1


def iota(shape, axis):
    return lax.broadcasted_iota(jnp.int32, shape, axis)


def place():
    return lax.axis_index("grp"), lax.axis_index("dev")


def fetch(pairs, sems):
    copies = [pltpu.make_async_copy(src, dst, sems.at[i]) for i, (src, dst) in enumerate(pairs)]
    for copy in copies:
        copy.start()
    for copy in copies:
        copy.wait()


def thirds(value):
    first = value.astype(jnp.bfloat16)
    rest = value - first.astype(jnp.float32)
    second = rest.astype(jnp.bfloat16)
    return first, second, (rest - second.astype(jnp.float32)).astype(jnp.bfloat16)


def dot(a, b):
    return jnp.dot(a, b, preferred_element_type=jnp.float32)


def pack_kernel(*refs):
    q_ref, codes_ref, owner_ref, local_ref = refs[5:9]
    out_ref, codes_t, sems = refs[4], refs[9], refs[10]
    fetch(list(zip(refs[:4], refs[5:9])), sems)
    codes_t[...] = codes_ref[...].astype(jnp.float32).T
    owner, local = owner_ref[...], local_ref[...]
    diagonal = iota((C, C), 0) == iota((C, C), 1)
    row = jnp.zeros((1, LANE), jnp.float32)
    for q in range(QN):
        owner_col = jnp.sum(jnp.where(diagonal, owner[q : q + 1, :], 0), axis=1, keepdims=True)
        local_col = jnp.sum(jnp.where(diagonal, local[q : q + 1, :], 0), axis=1, keepdims=True)
        hit = owner_col + q * C == iota((C, LANE), 1)
        row += jnp.sum(
            jnp.where(hit, local_col.astype(jnp.float32), 0.0), axis=0, keepdims=True
        )
    for p in range(C):
        tile, core = (p // 16) * 4 + p % 4, p % 2
        base = p * ROWS
        for i in range(HALF):
            t = 2 * i + core
            out_ref[base + i * QN : base + (i + 1) * QN, :] = q_ref[:, t * LANE : (t + 1) * LANE]
        first = base + HALF * QN
        start = tile * SPT + p // 4 % 2 * SUB
        out_ref[first : first + SUB, :] = codes_t[start : start + SUB, :]
        out_ref[first + SUB : first + SUB + 1, :] = row


def owner_kernel(codes_ref, other_ref, book_ref, docs_ref, other_docs_ref, out_ref, book_t, codes_t):
    core = lax.rem(lax.axis_index("dev"), 2)

    def put(i, column, value):
        for level, part in enumerate(thirds(value)):
            out_ref[level, i * LANE : (i + 1) * LANE, column * LANE : (column + 1) * LANE] = part

    for block, ref in enumerate((codes_ref, other_ref)):
        codes_t[block * M : (block + 1) * M, :] = ref[...].T
    for i in range(HALF):
        t = 2 * i + core
        columns = pl.ds(pl.multiple_of(t * LANE, LANE), LANE)
        for block, ref in enumerate((docs_ref, other_docs_ref)):
            put(i, block, ref[:, columns].T)
        book_t[0] = book_ref[:LANE, columns].T
        book_t[1] = book_ref[LANE:, columns].T
        for block in range(2):
            first = pl.multiple_of(block * M + t * SPT, SPT)
            rows = codes_t[pl.ds(first, SPT), :]
            made = []
            for m in range(SPT):
                code = jnp.broadcast_to(rows[m : m + 1, :], (SUB, LANE))
                index = lax.bitwise_and(code, LANE - 1)
                low = jnp.take_along_axis(book_t[0, m * SUB : (m + 1) * SUB, :], index, axis=1)
                high = jnp.take_along_axis(book_t[1, m * SUB : (m + 1) * SUB, :], index, axis=1)
                made.append(jnp.where(code >= LANE, high, low))
            put(i, 2 + block, jnp.concatenate(made, axis=0))


def query_rows(got_ref, row):
    return jnp.concatenate([got_ref[pl.ds(row + q, C, stride=ROWS), :] for q in range(QN)], axis=0)


def score_kernel(got_ref, table_ref, out_ref, codes_ref):
    group, dev = place()
    me = group * 16 + dev
    core = lax.rem(dev, 2)
    query = jnp.concatenate([query_rows(got_ref, i * QN) for i in range(HALF)], axis=1)
    q0, q1, q2 = thirds(query)
    t0, t1, t2 = table_ref[0], table_ref[1], table_ref[2]
    by_first = dot(jnp.concatenate([q0, q1, q2], axis=0), t0)
    by_second = dot(jnp.concatenate([q0, q1], axis=0), t1)
    scores = dot(q0, t2) + by_first[2 * LANE :] + by_second[LANE:]
    scores = scores + (by_second[:LANE] + by_first[LANE : 2 * LANE])
    scores = scores + by_first[:LANE]
    asked = got_ref[pl.ds(ROWS - 1, C, stride=ROWS), :]
    lanes = iota((C, LANE), 1)
    wide = iota((LANE, LANE), 1)
    diagonal = iota((LANE, LANE), 0) == wide
    rows = []
    for block in range(2):
        owner = me if block == 0 else me + 1 - 2 * core
        local = jnp.concatenate(
            [
                jnp.sum(jnp.where(lanes == q * C + owner, asked, 0.0), axis=1, keepdims=True)
                for q in range(QN)
            ],
            axis=0,
        ).astype(jnp.int32)
        hit = wide == local
        for kind in range(2):
            first = (kind * 2 + block) * LANE
            column = jnp.sum(
                jnp.where(hit, scores[:, first : first + LANE], 0.0), axis=1, keepdims=True
            )
            rows.append(jnp.sum(jnp.where(diagonal, column, 0.0), axis=0, keepdims=True))
    mine = jnp.concatenate(rows, axis=0)
    for p in range(C):
        out_ref[p] = mine
        first = p * ROWS + HALF * QN
        codes_ref[p] = got_ref[first : first + SUB, :]


def pair_kernel(got_ref, near_ref, z_ref, x_ref, both_ref, out_ref, query_ref):
    group, dev = place()
    across = lax.rem(lax.div(dev, 2), 2)
    own = lax.rem(lax.div(dev, 4), 2)
    asked = got_ref[pl.ds(ROWS - 1, C, stride=ROWS), :]
    asked = jnp.concatenate([asked, jnp.zeros((LANE - C, LANE), jnp.float32)], axis=0).T
    local = jnp.concatenate([asked[q * C : (q + 1) * C, :C] for q in range(QN)], axis=1)
    local = local.astype(jnp.int32)
    for tile in range(2):
        first, second, _ = thirds(query_rows(got_ref, (group * 2 + tile) * QN))
        for rows in (slice(0, LANE), slice(LANE, 2 * LANE)):
            query_ref[tile, rows, :LANE] = first
            query_ref[tile, rows, LANE:] = second
    at = [
        pl.ds(pl.multiple_of(tile * SPT + part * SUB, SUB), SUB)
        for tile in (across, 1 - across)
        for part in (own, 1 - own)
    ]
    for o in range(C):
        index = jnp.broadcast_to(local[o : o + 1, :], (SUB, LANE))
        for rows, ref in zip(at, (near_ref, z_ref, x_ref, both_ref)):
            out_ref[o, rows, :] = jnp.take_along_axis(ref[o], index, axis=1)


def log_parts(scores):
    top = jnp.max(scores, axis=0, keepdims=True)
    shifted = scores - top
    powers = jnp.exp(shifted)
    total = jnp.sum(powers, axis=0, keepdims=True)
    return powers / total, shifted - jnp.log(total)


def block(first, weight, pairs_ref, query_ref, table, out_ref):
    words = [
        (iota((SUB, LANE), 0) + (first + v * SUB)).astype(jnp.float32) for v in range(BLOCK // SUB)
    ]

    @pl.loop(0, 2 * SPT // TOGETHER)
    def _(step):
        total = [[jnp.zeros((SUB, LANE), jnp.float32)] * len(words) for _ in range(TOGETHER)]
        for o in range(C):
            part = weight[o]
            for i in range(TOGETHER):
                row = pairs_ref[o, pl.ds(step * TOGETHER + i, 1), :]
                code = jnp.broadcast_to(row, (SUB, LANE))
                for v, word in enumerate(words):
                    total[i][v] += jnp.where(code == word, part, 0.0)
        rows = pl.ds(pl.multiple_of(step * (TOGETHER * BLOCK), TOGETHER * BLOCK), TOGETHER * BLOCK)
        first, second, _ = thirds(jnp.concatenate(sum(total, []), axis=0))
        table[rows, :LANE] = first
        table[rows, LANE:] = second

    subspace = lax.div(iota((BLOCK, LANE), 1), SUB)
    for tile in range(2):
        base = tile * SPT * BLOCK
        product = dot(table[base : base + SPT * BLOCK, :], query_ref[tile])
        product = product[:, :LANE] + product[:, LANE:]
        result = jnp.zeros((BLOCK, LANE), jnp.float32)
        for m in range(SPT):
            rows = product[m * BLOCK : (m + 1) * BLOCK, :]
            result += jnp.where(subspace == m, rows, 0.0)
        out_ref[:, tile * LANE : (tile + 1) * LANE] = result


def there_kernel(scores_ref, pairs_ref, query_ref, out_ref, weight_ref, loss_ref, table):
    dev = lax.axis_index("dev")
    odd = lax.rem(iota((C, LANE), 0), 2) == 1

    def joined(mine, other):
        swapped = jnp.where(odd, pltpu.roll(other, 1, 0), pltpu.roll(other, C - 1, 0))
        return mine + swapped

    exact = joined(scores_ref[:, 0, :], scores_ref[:, 2, :])
    student = joined(scores_ref[:, 1, :], scores_ref[:, 3, :])
    teacher, log_teacher = log_parts(exact)
    soft, log_soft = log_parts(student)
    loss = jnp.sum(teacher * (log_teacher - log_soft), axis=0, keepdims=True)
    loss_ref[...] = loss
    share = soft - teacher
    for o in range(C):
        weight_ref[o] = jnp.broadcast_to(share[o : o + 1, :], (SUB, LANE))
    block((dev ^ 1) * BLOCK, weight_ref, pairs_ref, query_ref, table, out_ref)


def here_kernel(weight_ref, loss_ref, pairs_ref, query_ref, out_ref, own_loss_ref, table):
    group, dev = place()
    mine = iota((SUB, LANE), 1) == iota((SUB, LANE), 0) * C + (group * 16 + dev)
    picked = jnp.sum(jnp.where(mine, loss_ref[...], 0.0), axis=1, keepdims=True)
    for q in range(QN):
        own_loss_ref[q] = picked[q, 0]
    block(lax.axis_index("dev") * BLOCK, weight_ref, pairs_ref, query_ref, table, out_ref)


def vmem(n):
    return [pl.BlockSpec(memory_space=pltpu.VMEM)] * n


def call(kernel, outs, n_in, scratch=(), out_specs=None, flops=0, moved=0, space=pltpu.VMEM, mib=8):
    return pl.pallas_call(
        kernel,
        out_shape=outs,
        in_specs=[pl.BlockSpec(memory_space=space)] * n_in,
        out_specs=out_specs,
        scratch_shapes=list(scratch),
        compiler_params=pltpu.CompilerParams(vmem_limit_bytes=mib * 1024 * 1024),
        cost_estimate=pl.CostEstimate(flops=flops, bytes_accessed=moved, transcendentals=0),
    )


def f32(*shape):
    return jax.ShapeDtypeStruct(shape, jnp.float32)


def by_xor(value, bits, count):
    return lax.ppermute(value, "dev", [(i, i ^ bits) for i in range(count)])


def shards_once(queries, documents, doc_codes, codebook, candidate_owner, candidate_local):
    owners = lax.axis_size("dev")
    everyone = ("grp", "dev")
    other_docs = by_xor(documents, 1, owners)
    other_codes = by_xor(doc_codes, 1, owners)
    sent = call(
        pack_kernel,
        f32(C * ROWS, LANE),
        4,
        [
            pltpu.VMEM((QN, D), jnp.float32),
            pltpu.VMEM((LANE, M), jnp.int32),
            pltpu.VMEM((QN, C), jnp.int32),
            pltpu.VMEM((QN, C), jnp.int32),
            pltpu.VMEM((M, LANE), jnp.float32),
            pltpu.SemaphoreType.DMA((4,)),
        ],
        vmem(1)[0],
        0,
        1 << 20,
        pl.ANY,
        62,
    )(queries, doc_codes, candidate_owner, candidate_local)
    got = lax.all_to_all(
        sent.reshape(C, ROWS, 1, LANE), everyone, split_axis=0, concat_axis=0, tiled=True
    ).reshape(C * ROWS, LANE)
    table = call(
        owner_kernel,
        jax.ShapeDtypeStruct((3, HALF * LANE, 4 * LANE), jnp.bfloat16),
        5,
        [pltpu.VMEM((2, LANE, LANE), jnp.float32), pltpu.VMEM((2 * M, LANE), jnp.int32)],
        vmem(1)[0],
        1 << 22,
        1 << 21,
    )(doc_codes, other_codes, codebook, documents, other_docs)
    scores, codes = call(
        score_kernel, (f32(C, 4, LANE), f32(C, SUB, LANE)), 2, (), tuple(vmem(2)), 1 << 27, 1 << 21
    )(got, table)
    all_scores = lax.all_to_all(scores, everyone, split_axis=0, concat_axis=0, tiled=True)
    pairs, columns = call(
        pair_kernel,
        (f32(C, 2 * SPT, LANE), jax.ShapeDtypeStruct((2, 2 * LANE, 2 * LANE), jnp.bfloat16)),
        5,
        (),
        tuple(vmem(2)),
        1 << 20,
        1 << 20,
    )(got, codes, *[by_xor(codes, bits, owners) for bits in (4, 2, 6)])
    built = [pltpu.VMEM((2 * SPT * BLOCK, 2 * LANE), jnp.bfloat16)]
    there, weight, losses = call(
        there_kernel,
        (f32(BLOCK, 2 * LANE), f32(C, SUB, LANE), f32(1, LANE)),
        3,
        built,
        tuple(vmem(3)),
        1 << 27,
        1 << 21,
    )(all_scores, pairs, columns)
    far = by_xor(there, 1, owners)
    here, query_loss = call(
        here_kernel,
        (f32(BLOCK, 2 * LANE), f32(QN)),
        4,
        built,
        (vmem(1)[0], pl.BlockSpec(memory_space=pltpu.SMEM)),
        1 << 27,
        1 << 21,
    )(weight, losses, pairs, columns)
    odd = lax.rem(lax.axis_index("dev"), 2) == 1
    even, later = jnp.where(odd, far, here), jnp.where(odd, here, far)
    gradient = jnp.concatenate(
        [even[:, :LANE], later[:, :LANE], even[:, LANE:], later[:, LANE:]], axis=1
    )
    return gradient, query_loss


def slot_positions(candidate_owner, capacity):
    owner_flat = candidate_owner.reshape(-1)
    ordinal = jnp.arange(owner_flat.shape[0], dtype=jnp.int32)
    earlier = (owner_flat[None, :] == owner_flat[:, None]) & (ordinal[None, :] < ordinal[:, None])
    rank_inside = jnp.sum(earlier.astype(jnp.int32), axis=1)
    return owner_flat * capacity + rank_inside


def distill(exact_score, student):
    teacher = jax.nn.softmax(exact_score, axis=-1)
    query_loss = jnp.sum(
        teacher * (jax.nn.log_softmax(exact_score, axis=-1) - jax.nn.log_softmax(student, axis=-1)),
        axis=-1,
    )
    weight = jax.nn.softmax(student, axis=-1) - teacher
    return (query_loss, weight)


def code_onehot(code_block):
    return (code_block[:, :, None] == jnp.arange(K, dtype=jnp.int32)[None, None, :]).astype(
        jnp.float32
    )


def fetched_terms(queries, vectors, code_rows, codebook):
    query_count = queries.shape[0]
    exact_score = jnp.einsum("qcd,qd->qc", vectors, queries, precision=lax.Precision.HIGHEST)
    query_parts = queries.reshape(query_count, M, SUB)
    lookup = jnp.einsum(
        "qmj,kmj->qmk", query_parts, codebook.reshape(K, M, SUB), precision=lax.Precision.HIGHEST
    )

    def student_one(pieces):
        code_one, lookup_one = pieces
        return jnp.einsum(
            "cmk,mk->c", code_onehot(code_one), lookup_one, precision=lax.Precision.HIGHEST
        )

    student = lax.map(student_one, (code_rows, lookup))
    query_loss, weight = distill(exact_score, student)

    def table_one(pieces):
        code_one, weight_one = pieces
        return jnp.einsum(
            "cmk,c->mk", code_onehot(code_one), weight_one, precision=lax.Precision.HIGHEST
        )

    weight_table = lax.map(table_one, (code_rows, weight))
    gradient = jnp.einsum(
        "qmk,qmj->kmj", weight_table, query_parts, precision=lax.Precision.HIGHEST
    )
    return (query_loss, gradient.reshape(K, D))


def shards_any(queries, documents, doc_codes, codebook, candidate_owner, candidate_local):
    groups = lax.axis_size("grp")
    owners = lax.axis_size("dev")
    query_count = queries.shape[0]
    capacity = min(query_count, max(2, 2 * query_count * C // (groups * owners)))
    slot_count = groups * owners * capacity
    positions = slot_positions(candidate_owner, capacity)
    wanted = jnp.zeros((slot_count,), jnp.int32).at[positions].set(candidate_local.reshape(-1))
    asked = lax.all_to_all(
        lax.all_to_all(
            wanted.reshape(groups, owners, capacity), "grp", split_axis=0, concat_axis=0, tiled=True
        ),
        "dev",
        split_axis=1,
        concat_axis=1,
        tiled=True,
    )
    doc_index = asked.reshape(slot_count)
    found_rows = documents[doc_index].reshape(groups, owners, capacity, D)
    found_codes = doc_codes[doc_index].astype(jnp.float32).reshape(groups, owners, capacity, M)
    fetched, fetched_codes = (
        lax.all_to_all(
            lax.all_to_all(found_rows, "grp", split_axis=0, concat_axis=0, tiled=True),
            "dev",
            split_axis=1,
            concat_axis=1,
            tiled=True,
        ),
        lax.all_to_all(
            lax.all_to_all(found_codes, "grp", split_axis=0, concat_axis=0, tiled=True),
            "dev",
            split_axis=1,
            concat_axis=1,
            tiled=True,
        ),
    )
    vectors = fetched.reshape(slot_count, D)[positions].reshape(query_count, C, D)
    code_rows = (
        fetched_codes.reshape(slot_count, M)[positions].astype(jnp.int32).reshape(query_count, C, M)
    )
    query_loss, local_gradient = fetched_terms(queries, vectors, code_rows, codebook)
    partial_sum = lax.psum_scatter(local_gradient, "dev", scatter_dimension=0, tiled=True)
    codebook_gradient = lax.psum_scatter(partial_sum, "grp", scatter_dimension=1, tiled=True)
    return (codebook_gradient, query_loss)


def solution(mesh):
    in_specs = (
        P(("grp", "dev"), None),
        P(("grp", "dev"), None),
        P(("grp", "dev"), None),
        P(),
        P(("grp", "dev"), None),
        P(("grp", "dev"), None),
    )
    out_specs = (P("dev", "grp"), P(("grp", "dev")))

    def shards(queries, documents, *rest):
        once = dict(mesh.shape) == {"grp": 2, "dev": 16}
        once = once and queries.shape == (QN, D) and documents.shape == (LANE, D)
        return (shards_once if once else shards_any)(queries, documents, *rest)

    return jax.shard_map(shards, mesh=mesh, in_specs=in_specs, out_specs=out_specs, check_vma=False)
```
